512 devices in a mesh: tm: 64 (over z_lo, y, core), band: 8 (over z_hi, x).
Axes of the slice: x: 4, y: 8, z: 8 (z_hi: 2, z_lo: 4; z = z_hi * 4 + z_lo), core: 2. Of those that a mesh axis runs over, the one named last changes fastest.
Arguments:
- feats: bfloat16 [64, 64, 128, 256], P('tm', 'band'), may hold values from -6 to 6
- cotangent: bfloat16 [64, 64, 128, 256], P('tm', 'band'), may hold values from -6 to 6
- w_value: bfloat16 [256, 256], replicated, may hold values from -0.375 to 0.375
- w_logit: bfloat16 [256, 48], replicated, may hold values from -24 to 24
- w_out: bfloat16 [256, 256], replicated, may hold values from -0.375 to 0.375
- row_offsets: int32 [64, 5, 64, 128], P('tm', None, 'band'), may hold values from -1 to 0
- col_offsets: int32 [64, 5, 64, 128], P('tm', None, 'band'), may hold values from -8 to 7
- fractions: int32 [64, 2, 5, 64, 128], P('tm', None, None, 'band'), may hold values from 0 to 7
- present: int32 [64, 5], P('tm'), may hold values 0 or 1
Outputs:
- grad_feats: bfloat16 [64, 64, 128, 256], P('tm', 'band')
- grad_w_value: float32 [256, 256], replicated
- grad_w_logit: float32 [256, 48], replicated
- grad_w_out: float32 [256, 256], replicated
The draws below stay inside these ranges and needn't reach their ends.
All inputs are finite; a program needn't handle non-finite values. No bound on the sum of `present` on one device may be relied on, other than what follows from the above.
Results may differ from the reference program's by a relative error of at most 0.014.
Values may be sent and summed in bfloat16 or wider, within the bound.
No kernel may reach another device: no remote copies, remote signals or barrier semaphores. Data moves between devices by JAX's collectives and lax.ppermute only.
A program may use at most 64 MiB of HBM per device.

```python
import jax
import jax.numpy as jnp
from jax import lax

COLS = 128
C = 256
H = 8
E = 32
K = 5
J = 6
REACH = 1
COL_REACH = 8
FRAMES = 64
NROWS = 64


def draw_w_logit(key, part):
    first = jax.random.fold_in(key, 0)
    base = jnp.clip(jax.random.normal(first, (C, H * J), jnp.float32), -6.0, 6.0) * C ** (-0.5)
    return base.astype(jnp.bfloat16)


def set_ends(drawn, rng, low, top_value):
    longest = drawn.shape.index(max(drawn.shape))
    spots = []
    for shift in (0, 1):
        where = [jax.random.randint(jax.random.fold_in(rng, axis), (), 0, length) for axis, length in enumerate(drawn.shape)]
        where[longest] = (where[longest] + shift) % drawn.shape[longest]
        spots.append(tuple(where))
    return drawn.at[spots[0]].set(low).at[spots[1]].set(top_value)


def level_of(rng, shape, pieces, least, high):
    def one(dim, blocks):
        steps = jax.random.uniform(jax.random.fold_in(jax.random.fold_in(rng, 6), dim), (blocks,), jnp.float32, least / len(pieces), high / len(pieces))
        return jnp.repeat(jnp.exp(steps), shape[dim] // blocks).reshape((-1,) + (1,) * (len(shape) - dim - 1))

    loudness = one(*pieces[0])
    for cut in pieces[1:]:
        loudness = loudness * one(*cut)
    return loudness


def scatter_about(stream_key, dims, spread, limit, cuts=(), kind=jnp.bfloat16):
    array = spread * jax.random.normal(stream_key, dims, jnp.float32)
    if cuts:
        array = array * level_of(stream_key, dims, cuts, -0.22, 0.18)
    return jnp.clip(array, -limit, limit).astype(kind)


def setup_inputs(seed: int = 0) -> dict:
    arg_keys = jax.random.split(jax.random.key(seed), 10)
    feats = scatter_about(arg_keys[0], (FRAMES, NROWS, COLS, C), 1.0, 6.0, ((0, 64), (1, 8)))
    cotangent = scatter_about(arg_keys[1], (FRAMES, NROWS, COLS, C), 1.0, 6.0, ((0, 64), (1, 8)))
    w_value = scatter_about(arg_keys[2], (C, C), C ** -0.5, 0.375)
    w_logit = draw_w_logit(jax.random.fold_in(arg_keys[9], 71), 0)
    w_out = scatter_about(arg_keys[4], (C, C), C ** -0.5, 0.375)
    row_offsets = set_ends(jax.random.randint(arg_keys[5], (FRAMES, K, NROWS, COLS), -REACH, REACH), jax.random.fold_in(arg_keys[5], 1), -REACH, REACH - 1).astype(jnp.int32)
    col_offsets = set_ends(jax.random.randint(arg_keys[6], (FRAMES, K, NROWS, COLS), -COL_REACH, COL_REACH), jax.random.fold_in(arg_keys[6], 1), -COL_REACH, COL_REACH - 1).astype(jnp.int32)
    fractions = set_ends(jax.random.randint(arg_keys[7], (FRAMES, 2, K, NROWS, COLS), 0, 8), jax.random.fold_in(arg_keys[7], 1), 0, 7).astype(jnp.int32)
    present = set_ends((jax.random.randint(arg_keys[8], (FRAMES, K), 0, 8) < 7).astype(jnp.int32), jax.random.fold_in(arg_keys[8], 1), 0, 1)
    return dict(feats=feats, cotangent=cotangent, w_value=w_value, w_logit=w_logit, w_out=w_out, row_offsets=row_offsets, col_offsets=col_offsets, fractions=fractions, present=present)


DISTANCES = (1, 2, 4, 8, 16)


def corner_list(row_shift, col_shift, row_frac, col_frac, row_here, col_here, column_count, reach_rows):
    result = []
    for row_step in (0, 1):
        if row_step == 0:
            row_weight = 8 - row_frac
        else:
            row_weight = row_frac
        for col_step in (0, 1):
            if col_step == 0:
                col_weight = 8 - col_frac
            else:
                col_weight = col_frac
            ext_row = row_here + row_shift + row_step + reach_rows
            ext_col = col_here + col_shift + col_step
            inside = (ext_col >= 0) & (ext_col < column_count)
            target = (ext_row * column_count + jnp.clip(ext_col, 0, column_count - 1)).astype(jnp.int32)
            weight = jnp.where(inside, (row_weight * col_weight).astype(jnp.float32) / 64.0, jnp.float32(0.0))
            result.append((target, weight))
    return result


def reference(feats, cotangent, w_value, w_logit, w_out, row_offsets, col_offsets, fractions, present):
    frames = feats.shape[0]
    grid_rows = feats.shape[1]
    column_count = feats.shape[2]
    channels = feats.shape[3]
    cells = grid_rows * column_count
    padded_rows = grid_rows + 2 * REACH
    flat_in = feats.reshape(frames * cells, channels)
    flat_grad = cotangent.reshape(frames * cells, channels)
    values = jnp.dot(flat_in, w_value, preferred_element_type=jnp.float32).astype(jnp.bfloat16)
    values_frames = values.reshape(frames, cells, channels)
    padded = jnp.pad(values.reshape(frames, grid_rows, column_count, channels), ((0, 0), (REACH, REACH), (0, 0), (0, 0)))
    padded = padded.reshape(frames, padded_rows * column_count, channels)
    logits_all = jnp.dot(flat_in, w_logit, preferred_element_type=jnp.float32).reshape(frames, cells, H, J)
    grad_frames = cotangent.reshape(frames, cells, channels)
    cell_index = jnp.arange(cells, dtype=jnp.int32)
    row_here = cell_index // column_count
    col_here = cell_index % column_count

    def step(accum, frame_index):
        sampled = [values_frames[frame_index]]
        corner_sets = []
        valid = [jnp.asarray(True)]
        for slot in range(K):
            distance = DISTANCES[slot]
            source = jnp.maximum(frame_index - distance, 0)
            reached = frame_index >= distance
            valid.append(reached & (present[frame_index, slot] == 1))
            block = padded[source]
            sets = corner_list(row_offsets[frame_index, slot].reshape(cells), col_offsets[frame_index, slot].reshape(cells),
                               fractions[frame_index, 0, slot].reshape(cells), fractions[frame_index, 1, slot].reshape(cells),
                               row_here, col_here, column_count, REACH)
            total = jnp.zeros((cells, channels), jnp.float32)
            for target, weight in sets:
                total = total + weight[:, None] * block[target].astype(jnp.float32)
            total = jnp.where(reached, total, jnp.float32(0.0))
            sampled.append(total.astype(jnp.bfloat16))
            corner_sets.append(sets)
        valid_vec = jnp.stack(valid)
        logits = logits_all[frame_index]
        masked = jnp.where(valid_vec[None, None, :], logits, jnp.float32(-1e30))
        top = jnp.max(masked, axis=2, keepdims=True)
        expo = jnp.where(valid_vec[None, None, :], jnp.exp(masked - top), jnp.float32(0.0))
        attn = expo / jnp.sum(expo, axis=2, keepdims=True)
        attn_low = attn.astype(jnp.bfloat16)
        stacked = jnp.stack(sampled).reshape(J, cells, H, E)
        mixed = jnp.einsum("qhj,jqhe->qhe", attn_low.astype(jnp.float32), stacked.astype(jnp.float32))
        mixed = mixed.reshape(cells, channels).astype(jnp.bfloat16)
        d_mixed = jnp.dot(grad_frames[frame_index], w_out.T, preferred_element_type=jnp.float32).astype(jnp.bfloat16)
        d_heads = d_mixed.reshape(cells, H, E).astype(jnp.float32)
        d_attn = jnp.einsum("qhe,jqhe->qhj", d_heads, stacked.astype(jnp.float32))
        d_logits = attn * (d_attn - jnp.sum(attn * d_attn, axis=2, keepdims=True))
        d_logit_low = d_logits.reshape(cells, H * J).astype(jnp.bfloat16)
        d_sampled = jnp.einsum("qhj,qhe->jqhe", attn_low.astype(jnp.float32), d_heads).astype(jnp.bfloat16)
        d_sampled = d_sampled.reshape(J, cells, channels)
        self_term = jnp.pad(d_sampled[0].astype(jnp.float32).reshape(grid_rows, column_count, channels),
                            ((REACH, REACH), (0, 0), (0, 0))).reshape(padded_rows * column_count, channels)
        accum = accum.at[frame_index].add(self_term)
        for slot in range(K):
            distance = DISTANCES[slot]
            source = jnp.maximum(frame_index - distance, 0)
            contrib = jnp.zeros((padded_rows * column_count, channels), jnp.float32)
            grad_slot = d_sampled[slot + 1].astype(jnp.float32)
            for target, weight in corner_sets[slot]:
                contrib = contrib.at[target].add(weight[:, None] * grad_slot)
            accum = accum.at[source].add(contrib)
        return accum, (mixed, d_logit_low)

    start = jnp.zeros((frames, padded_rows * column_count, channels), jnp.float32)
    accum, (mixed_all, dlog_all) = lax.scan(step, start, jnp.arange(frames, dtype=jnp.int32))
    dvalues = accum.reshape(frames, padded_rows, column_count, channels)[:, REACH:REACH + grid_rows]
    dvalues = dvalues.reshape(frames * cells, channels).astype(jnp.bfloat16)
    dlog_flat = dlog_all.reshape(frames * cells, H * J)
    grad_w_out = jnp.dot(mixed_all.reshape(frames * cells, channels).T, flat_grad, preferred_element_type=jnp.float32)
    grad_w_value = jnp.dot(flat_in.T, dvalues, preferred_element_type=jnp.float32)
    grad_w_logit = jnp.dot(flat_in.T, dlog_flat, preferred_element_type=jnp.float32)
    grad_in = flat_grad.astype(jnp.float32) + jnp.dot(dvalues, w_value.T, preferred_element_type=jnp.float32)
    grad_in = grad_in + jnp.dot(dlog_flat, w_logit.T, preferred_element_type=jnp.float32)
    grad_feats = grad_in.astype(jnp.bfloat16).reshape(feats.shape)
    return (grad_feats, grad_w_value, grad_w_logit, grad_w_out)
```

```python
import jax
import jax.numpy as jnp
from jax import lax
from jax.experimental import pallas as pl
from jax.experimental.pallas import tpu as pltpu
from jax.sharding import PartitionSpec as P

H = 8
E = 32
K = 5
J = 6
C = 256
COLS = 128
ROWS = 8
CELLS = ROWS * COLS
EXT = CELLS + 2 * COLS
PAY = 384
DISTANCES = (1, 2, 4, 8, 16)

F32 = jnp.float32
BF16 = jnp.bfloat16


def mm(a, b, ca, cb):
    return lax.dot_general(a, b, (((ca,), (cb,)), ((), ())), preferred_element_type=F32)


def iota(shape, dim):
    return lax.broadcasted_iota(jnp.int32, shape, dim)


def head_spread():
    return jnp.where(iota((H, C), 1) // E == iota((H, C), 0), 1.0, 0.0).astype(BF16)


def head_sums(spread, prod):
    high = prod.astype(BF16)
    low = (prod - high.astype(F32)).astype(BF16)
    return mm(spread, high, 1, 1) + mm(spread, low, 1, 1)


def rows_of(r):
    return pl.ds(r * COLS, COLS)


def prep_body(
    present, feats, cot, w_value, w_logit, w_out, row_off, col_off, fracs,
    values, attn, packets, dattn, accum, gwo, wl_t, mix,
):
    frame = lax.axis_index("tm")
    r48 = iota((H * J, H * J), 0)
    c48 = iota((H * J, H * J), 1)
    order = jnp.where(c48 == (r48 % H) * J + r48 // H, 1.0, 0.0).astype(BF16)
    wl = mm(order, w_logit[...], 1, 1).astype(BF16)
    wl_t[...] = wl
    spread = head_spread()
    valid = [None]
    for k in range(K):
        valid.append((present[0, k] == 1) & (frame >= DISTANCES[k]))
    accum[pl.ds(0, COLS), :] = jnp.zeros((COLS, C), F32)
    accum[pl.ds(EXT - COLS, COLS), :] = jnp.zeros((COLS, C), F32)
    for r in range(ROWS):
        f = feats[rows_of(r), :]
        v = mm(f, w_value[...], 1, 0).astype(BF16)
        values[rows_of(r), :] = v
        logits = mm(wl, f, 1, 1)
        masked = [logits[0:H]]
        for k in range(K):
            part = logits[(k + 1) * H : (k + 2) * H]
            masked.append(jnp.where(valid[k + 1], part, -1e30))
        top = masked[0]
        for part in masked[1:]:
            top = jnp.maximum(top, part)
        expo = [jnp.exp(masked[0] - top)]
        for k in range(K):
            expo.append(jnp.where(valid[k + 1], jnp.exp(masked[k + 1] - top), 0.0))
        total = expo[0]
        for part in expo[1:]:
            total = total + part
        weights = [part / total for part in expo]
        attn[:, rows_of(r)] = jnp.concatenate(weights, axis=0)
        for k in range(K):
            head = jnp.concatenate(
                [
                    weights[k + 1],
                    col_off[k, r : r + 1, :].astype(F32),
                    row_off[k, r : r + 1, :].astype(F32),
                    fracs[0, k, r : r + 1, :].astype(F32),
                    fracs[1, k, r : r + 1, :].astype(F32),
                    jnp.zeros((4, COLS), F32),
                ],
                axis=0,
            )
            packets[k, :, rows_of(r)] = head.astype(BF16)
        wide = mm(weights[0].astype(BF16), spread, 0, 0)
        dm = mm(cot[rows_of(r), :], w_out[...], 1, 1).astype(BF16).astype(F32)
        vf = v.astype(F32)
        dattn[:, rows_of(r)] = head_sums(spread, dm * vf)
        accum[rows_of(r + 1), :] = (wide * dm).astype(BF16).astype(F32)
        mix[rows_of(r), :] = (wide * vf).astype(BF16)
    gwo[...] = mm(mix[...], cot[...], 0, 0)


def slot_body(cot, packet, ext, w_out, accum_in, gwo_in, dattn, accum, gwo, mix):
    spread = head_spread()
    src = iota((COLS, COLS), 0).astype(F32)
    lane = iota((1, COLS), 1).astype(F32)
    accum[...] = accum_in[...]
    for r in range(ROWS):
        pack = packet[:, rows_of(r)]
        info = pack[8:16].astype(F32)
        c0 = lane + info[0:1]
        up = info[1:2] < -0.5
        a = info[2:3] * (1.0 / 64.0)
        b = info[3:4]
        near = 0.125 - a
        columns = jnp.where(src == c0, 8.0 - b, 0.0) + jnp.where(src == c0 + 1.0, b, 0.0)
        w0 = jnp.where(up, near, 0.0)
        w1 = jnp.where(up, a, near)
        w2 = jnp.where(up, 0.0, a)
        table = jnp.concatenate(
            [(columns * w0).astype(BF16), (columns * w1).astype(BF16), (columns * w2).astype(BF16)],
            axis=0,
        )
        window = pl.ds(r * COLS, 3 * COLS)
        taken = mm(table, ext[window, :], 0, 0).astype(BF16).astype(F32)
        wide = mm(pack[0:H], spread, 0, 0)
        dm = mm(cot[rows_of(r), :], w_out[...], 1, 1).astype(BF16).astype(F32)
        dattn[:, rows_of(r)] = head_sums(spread, dm * taken)
        mix[rows_of(r), :] = (wide * taken).astype(BF16)
        accum[window, :] += mm(table, (wide * dm).astype(BF16), 1, 0)
    gwo[...] = gwo_in[...] + mm(mix[...], cot[...], 0, 0)


def final_body(
    feats, cot, w_value, wl_t, attn, d0, d1, d2, d3, d4, d5, accum, from_prev, from_next, gwo,
    grad_feats, pay, dv, dl_a, dl_b,
):
    grads = (d0, d1, d2, d3, d4, d5)
    r48 = iota((H * J, COLS), 0)
    c48 = iota((H * J, COLS), 1)
    column = (r48 % H) * J + r48 // H
    half = H * J // 2
    first = jnp.where((c48 < half) & (column == c48), 1.0, 0.0).astype(BF16)
    second = jnp.where((c48 < half) & (column == c48 + half), 1.0, 0.0).astype(BF16)
    for r in range(ROWS):
        center = accum[rows_of(r + 1), :]
        if r == 0:
            center = center + from_prev[...].astype(F32)
        if r == ROWS - 1:
            center = center + from_next[...].astype(F32)
        low = center.astype(BF16)
        dv[rows_of(r), :] = low
        weights = [attn[pl.ds(j * H, H), rows_of(r)] for j in range(J)]
        terms = [grads[j][:, rows_of(r)] for j in range(J)]
        mean = weights[0] * terms[0]
        for j in range(1, J):
            mean = mean + weights[j] * terms[j]
        dl = jnp.concatenate(
            [weights[j] * (terms[j] - mean) for j in range(J)], axis=0
        ).astype(BF16)
        dl_a[rows_of(r), :] = mm(dl, first, 0, 0).astype(BF16)
        dl_b[rows_of(r), :] = mm(dl, second, 0, 0).astype(BF16)
        out = cot[rows_of(r), :].astype(F32) + mm(low, w_value[...], 1, 1)
        out = out + mm(dl, wl_t[...], 0, 0)
        grad_feats[rows_of(r), :] = out.astype(BF16)
    pay[pl.ds(0, C), pl.ds(0, C)] = gwo[...]
    pay[pl.ds(C, C), pl.ds(0, C)] = mm(feats[...], dv[...], 0, 0)
    pay[pl.ds(0, C), pl.ds(C, COLS)] = mm(feats[...], dl_a[...], 0, 0)
    pay[pl.ds(C, C), pl.ds(C, COLS)] = mm(feats[...], dl_b[...], 0, 0)


VM = pl.BlockSpec(memory_space=pltpu.VMEM)
SM = pl.BlockSpec(memory_space=pltpu.SMEM)


def sds(shape, dtype):
    return jax.ShapeDtypeStruct(shape, dtype)


def cost(flops, nbytes):
    return pl.CostEstimate(flops=flops, bytes_accessed=nbytes, transcendentals=0)


PARAMS = pltpu.CompilerParams(vmem_limit_bytes=48 * 1024 * 1024)


def prep(present, feats, cot, w_value, w_logit, w_out, row_off, col_off, fracs):
    return pl.pallas_call(
        prep_body,
        name="prep",
        out_shape=(
            sds((CELLS, C), BF16),
            sds((H * J, CELLS), F32),
            sds((K, 16, CELLS), BF16),
            sds((H, CELLS), F32),
            sds((EXT, C), F32),
            sds((C, C), F32),
            sds((H * J, C), BF16),
        ),
        in_specs=[SM] + [VM] * 8,
        out_specs=(VM,) * 7,
        scratch_shapes=[pltpu.VMEM((CELLS, C), BF16)],
        compiler_params=PARAMS,
        cost_estimate=cost(10**9, 4 * 10**6),
    )(present, feats, cot, w_value, w_logit, w_out, row_off, col_off, fracs)


def slot_call(cot, packet, ext, w_out, accum, gwo):
    return pl.pallas_call(
        slot_body,
        name="slot",
        out_shape=(sds((H, CELLS), F32), sds((EXT, C), F32), sds((C, C), F32)),
        in_specs=[VM] * 6,
        out_specs=(VM,) * 3,
        scratch_shapes=[pltpu.VMEM((CELLS, C), BF16)],
        input_output_aliases={4: 1, 5: 2},
        compiler_params=PARAMS,
        cost_estimate=cost(10**9, 4 * 10**6),
    )(cot, packet, ext, w_out, accum, gwo)


def final(*args):
    return pl.pallas_call(
        final_body,
        name="final",
        out_shape=(sds((CELLS, C), BF16), sds((2 * C, PAY), F32)),
        in_specs=[VM] * 15,
        out_specs=(VM,) * 2,
        scratch_shapes=[
            pltpu.VMEM((CELLS, C), BF16),
            pltpu.VMEM((CELLS, COLS), BF16),
            pltpu.VMEM((CELLS, COLS), BF16),
        ],
        compiler_params=PARAMS,
        cost_estimate=cost(10**9, 4 * 10**6),
    )(*args)


def shifted(value, axis, steps):
    count = lax.axis_size(axis)
    initial, last = (max(0, -steps), min(count, count - steps))
    return lax.ppermute(value, axis, [(source, source + steps) for source in range(initial, last)])


def shards(feats, cotangent, w_value, w_logit, w_out, row_offsets, col_offsets, fractions, present):
    inputs = feats.reshape(CELLS, C)
    grad_out = cotangent.reshape(CELLS, C)
    cots = [shifted(grad_out, "tm", -d) for d in DISTANCES]
    values, attn, packets, d0, accum, gwo, wl_t = prep(
        present, inputs, grad_out, w_value, w_logit, w_out, row_offsets[0], col_offsets[0], fractions[0]
    )
    low = shifted(values[CELLS - COLS :], "band", 1)
    high = shifted(values[:COLS], "band", -1)
    ext = jnp.concatenate([low, values, high], axis=0)
    packs = [shifted(packets[k], "tm", -DISTANCES[k]) for k in range(K)]
    grads = [None] * K
    for k in (4, 0, 1, 2, 3):
        grads[k], accum, gwo = slot_call(cots[k], packs[k], ext, w_out, accum, gwo)
    back = [shifted(grads[k], "tm", DISTANCES[k]) for k in range(K)]
    from_next = shifted(accum[:COLS].astype(BF16), "band", -1)
    from_prev = shifted(accum[EXT - COLS :].astype(BF16), "band", 1)
    grad_feats, pay = final(
        inputs, grad_out, w_value, wl_t, attn, d0, *back, accum, from_prev, from_next, gwo
    )
    both = ("tm", "band")
    count = lax.axis_size("tm") * lax.axis_size("band")
    share = 2 * C // count
    pieces = lax.all_to_all(pay, both, 0, 0, tiled=True)
    mine = jnp.sum(pieces.reshape(count, share, PAY), axis=0)
    spread = jnp.broadcast_to(mine[None], (count, share, PAY)).reshape(2 * C, PAY)
    whole = lax.all_to_all(spread, both, 0, 0, tiled=True)
    half = H * J // 2
    gwl = jnp.concatenate([whole[:C, C : C + half], whole[C:, C : C + half]], axis=1)
    return (grad_feats.reshape(feats.shape), whole[C:, :C], gwl, whole[:C, :C])


def solution(mesh):
    placed = (
        P("tm", "band", None, None),
        P("tm", "band", None, None),
        P(),
        P(),
        P(),
        P("tm", None, "band", None),
        P("tm", None, "band", None),
        P("tm", None, None, "band", None),
        P("tm", None),
    )
    return jax.shard_map(
        shards,
        mesh=mesh,
        in_specs=placed,
        out_specs=(P("tm", "band", None, None), P(), P(), P()),
        check_vma=False,
    )
```

```python
import math

import jax
import numpy as np
import jax.numpy as jnp
from jax import lax
from jax.experimental import pallas as pl
from jax.experimental.pallas import tpu as pltpu
from jax.sharding import PartitionSpec as P


H = 8
E = 32
K = 5
J = 6
C = 256
COLS = 128
ROWS = 8
CELLS = ROWS * COLS
EXT = CELLS + 2 * COLS
PAY = 384
DISTANCES = (1, 2, 4, 8, 16)
SLOTS = (4, 1, 0, 2, 3)

TM = ("pair", "core")

F32 = jnp.float32
BF16 = jnp.bfloat16


def mm(a, b, ca, cb):
    return lax.dot_general(a, b, (((ca,), (cb,)), ((), ())), preferred_element_type=F32)


def iota(shape, dim):
    return lax.broadcasted_iota(jnp.int32, shape, dim)


def head_spread():
    return jnp.where(iota((H, C), 1) // E == iota((H, C), 0), 1.0, 0.0).astype(BF16)


def head_sums(spread, prod):
    high = prod.astype(BF16)
    low = (prod - high.astype(F32)).astype(BF16)
    return mm(spread, high, 1, 1) + mm(spread, low, 1, 1)


def rows_of(r):
    return pl.ds(r * COLS, COLS)


def prep_body(
    present, feats_hbm, cot_hbm, w_value_hbm, w_logit_hbm, w_out_hbm, row_hbm, col_hbm, fracs_hbm,
    values, attn, packets, dattn, accum, gwo, wl_t,
    mix, feats, cot, w_value, w_logit, w_out, row_off, col_off, fracs, sems,
):
    frame = lax.axis_index(TM)
    moves = (
        (w_logit_hbm, w_logit), (w_value_hbm, w_value), (feats_hbm, feats), (row_hbm, row_off),
        (col_hbm, col_off), (fracs_hbm, fracs), (w_out_hbm, w_out), (cot_hbm, cot),
    )
    copies = [pltpu.make_async_copy(src, dst, sems.at[i]) for i, (src, dst) in enumerate(moves)]
    for copy in copies:
        copy.start()
    for copy in copies:
        copy.wait()
    r48 = iota((H * J, H * J), 0)
    c48 = iota((H * J, H * J), 1)
    order = jnp.where(c48 == (r48 % H) * J + r48 // H, 1.0, 0.0).astype(BF16)
    wl = mm(order, w_logit[...], 1, 0).astype(BF16)
    wl_t[...] = wl
    spread = head_spread()
    valid = [None]
    for k in range(K):
        valid.append((present[0, k] == 1) & (frame >= DISTANCES[k]))
    accum[pl.ds(0, COLS), :] = jnp.zeros((COLS, C), F32)
    accum[pl.ds(EXT - COLS, COLS), :] = jnp.zeros((COLS, C), F32)
    for r in range(ROWS):
        f = feats[rows_of(r), :]
        v = mm(f, w_value[...], 1, 0).astype(BF16)
        values[rows_of(r), :] = v
        logits = mm(wl, f, 1, 1)
        masked = [logits[0:H]]
        for k in range(K):
            part = logits[(k + 1) * H : (k + 2) * H]
            masked.append(jnp.where(valid[k + 1], part, -1e30))
        top = masked[0]
        for part in masked[1:]:
            top = jnp.maximum(top, part)
        expo = [jnp.exp(masked[0] - top)]
        for k in range(K):
            expo.append(jnp.where(valid[k + 1], jnp.exp(masked[k + 1] - top), 0.0))
        total = expo[0]
        for part in expo[1:]:
            total = total + part
        weights = [part / total for part in expo]
        attn[:, rows_of(r)] = jnp.concatenate(weights, axis=0)
        for k in range(K):
            head = jnp.concatenate(
                [
                    weights[k + 1],
                    col_off[k, r : r + 1, :].astype(F32),
                    row_off[k, r : r + 1, :].astype(F32),
                    fracs[0, k, r : r + 1, :].astype(F32),
                    fracs[1, k, r : r + 1, :].astype(F32),
                    jnp.zeros((4, COLS), F32),
                ],
                axis=0,
            )
            packets[k, :, rows_of(r)] = head.astype(BF16)
        wide = mm(weights[0].astype(BF16), spread, 0, 0)
        dm = mm(cot[rows_of(r), :], w_out[...], 1, 1).astype(BF16).astype(F32)
        vf = v.astype(F32)
        dattn[:, rows_of(r)] = head_sums(spread, dm * vf)
        accum[rows_of(r + 1), :] = (wide * dm).astype(BF16).astype(F32)
        mix[rows_of(r), :] = (wide * vf).astype(BF16)
    gwo[...] = mm(mix[...], cot[...], 0, 0)


def slot_body(cot, packet, ext, w_out, accum_in, gwo_in, dattn, accum, gwo, mix):
    spread = head_spread()
    src = iota((COLS, COLS), 0).astype(F32)
    lane = iota((1, COLS), 1).astype(F32)
    accum[...] = accum_in[...]
    for r in range(ROWS):
        pack = packet[:, rows_of(r)]
        info = pack[8:16].astype(F32)
        c0 = lane + info[0:1]
        up = info[1:2] < -0.5
        a = info[2:3] * (1.0 / 64.0)
        b = info[3:4]
        near = 0.125 - a
        columns = jnp.where(src == c0, 8.0 - b, 0.0) + jnp.where(src == c0 + 1.0, b, 0.0)
        w0 = jnp.where(up, near, 0.0)
        w1 = jnp.where(up, a, near)
        w2 = jnp.where(up, 0.0, a)
        table = jnp.concatenate(
            [(columns * w0).astype(BF16), (columns * w1).astype(BF16), (columns * w2).astype(BF16)],
            axis=0,
        )
        window = pl.ds(r * COLS, 3 * COLS)
        taken = mm(table, ext[window, :], 0, 0).astype(BF16).astype(F32)
        wide = mm(pack[0:H], spread, 0, 0)
        dm = mm(cot[rows_of(r), :], w_out[...], 1, 1).astype(BF16).astype(F32)
        dattn[:, rows_of(r)] = head_sums(spread, dm * taken)
        mix[rows_of(r), :] = (wide * taken).astype(BF16)
        accum[window, :] += mm(table, (wide * dm).astype(BF16), 1, 0)
    gwo[...] = gwo_in[...] + mm(mix[...], cot[...], 0, 0)


def final_body(
    feats, cot, w_value, wl_t, attn, d0, d1, d2, d3, d4, d5, accum, from_prev, from_next, gwo,
    grad_feats, keep, send, dv, dl_a, dl_b,
):
    grads = (d0, d1, d2, d3, d4, d5)
    r48 = iota((H * J, COLS), 0)
    c48 = iota((H * J, COLS), 1)
    column = (r48 % H) * J + r48 // H
    half = H * J // 2
    first = jnp.where((c48 < half) & (column == c48), 1.0, 0.0).astype(BF16)
    second = jnp.where((c48 < half) & (column == c48 + half), 1.0, 0.0).astype(BF16)
    for r in range(ROWS):
        center = accum[rows_of(r + 1), :]
        if r == 0:
            center = center + from_prev[...].astype(F32)
        if r == ROWS - 1:
            center = center + from_next[...].astype(F32)
        low = center.astype(BF16)
        dv[rows_of(r), :] = low
        weights = [attn[pl.ds(j * H, H), rows_of(r)] for j in range(J)]
        terms = [grads[j][:, rows_of(r)] for j in range(J)]
        mean = weights[0] * terms[0]
        for j in range(1, J):
            mean = mean + weights[j] * terms[j]
        dl = jnp.concatenate(
            [weights[j] * (terms[j] - mean) for j in range(J)], axis=0
        ).astype(BF16)
        dl_a[rows_of(r), :] = mm(dl, first, 0, 0).astype(BF16)
        dl_b[rows_of(r), :] = mm(dl, second, 0, 0).astype(BF16)
        out = cot[rows_of(r), :].astype(F32) + mm(low, w_value[...], 1, 1)
        out = out + mm(dl, wl_t[...], 0, 0)
        grad_feats[rows_of(r), :] = out.astype(BF16)
    core = lax.axis_index("core")
    for mine in (0, 1):

        @pl.when(core == mine)
        def _():
            upper, lower = (keep, send) if mine == 0 else (send, keep)
            upper[:, pl.ds(0, C)] = gwo[...]
            upper[:, pl.ds(C, COLS)] = mm(feats[...], dl_a[...], 0, 0)
            lower[:, pl.ds(0, C)] = mm(feats[...], dv[...], 0, 0)
            lower[:, pl.ds(C, COLS)] = mm(feats[...], dl_b[...], 0, 0)


VM = pl.BlockSpec(memory_space=pltpu.VMEM)
SM = pl.BlockSpec(memory_space=pltpu.SMEM)
HB = pl.BlockSpec(memory_space=pltpu.HBM)


def sds(shape, dtype):
    return jax.ShapeDtypeStruct(shape, dtype)


def cost(flops, nbytes):
    return pl.CostEstimate(flops=flops, bytes_accessed=nbytes, transcendentals=0)


PARAMS = pltpu.CompilerParams(vmem_limit_bytes=48 * 1024 * 1024)


def prep(present, feats, cot, w_value, w_logit, w_out, row_off, col_off, fracs):
    return pl.pallas_call(
        prep_body,
        name="prep",
        out_shape=(
            sds((CELLS, C), BF16),
            sds((H * J, CELLS), F32),
            sds((K, 16, CELLS), BF16),
            sds((H, CELLS), F32),
            sds((EXT, C), F32),
            sds((C, C), F32),
            sds((H * J, C), BF16),
        ),
        in_specs=[SM] + [HB] * 8,
        out_specs=(VM,) * 7,
        scratch_shapes=[
            pltpu.VMEM((CELLS, C), BF16),
            pltpu.VMEM((CELLS, C), BF16),
            pltpu.VMEM((CELLS, C), BF16),
            pltpu.VMEM((C, C), BF16),
            pltpu.VMEM((H * J, C), BF16),
            pltpu.VMEM((C, C), BF16),
            pltpu.VMEM((K, ROWS, COLS), jnp.int32),
            pltpu.VMEM((K, ROWS, COLS), jnp.int32),
            pltpu.VMEM((2, K, ROWS, COLS), jnp.int32),
            pltpu.SemaphoreType.DMA((8,)),
        ],
        compiler_params=PARAMS,
        cost_estimate=cost(10**9, 4 * 10**6),
    )(
        present,
        *(
            pltpu.with_memory_space_constraint(x, pltpu.HBM)
            for x in (feats, cot, w_value, w_logit, w_out, row_off, col_off, fracs)
        ),
    )


def slot_call(cot, packet, ext, w_out, accum, gwo):
    return pl.pallas_call(
        slot_body,
        name="slot",
        out_shape=(sds((H, CELLS), F32), sds((EXT, C), F32), sds((C, C), F32)),
        in_specs=[VM] * 6,
        out_specs=(VM,) * 3,
        scratch_shapes=[pltpu.VMEM((CELLS, C), BF16)],
        input_output_aliases={4: 1, 5: 2},
        compiler_params=PARAMS,
        cost_estimate=cost(10**9, 4 * 10**6),
    )(cot, packet, ext, w_out, accum, gwo)


def final(*args):
    return pl.pallas_call(
        final_body,
        name="final",
        out_shape=(sds((CELLS, C), BF16), sds((C, PAY), F32), sds((C, PAY), F32)),
        in_specs=[VM] * 15,
        out_specs=(VM,) * 3,
        scratch_shapes=[
            pltpu.VMEM((CELLS, C), BF16),
            pltpu.VMEM((CELLS, COLS), BF16),
            pltpu.VMEM((CELLS, COLS), BF16),
        ],
        compiler_params=PARAMS,
        cost_estimate=cost(10**9, 4 * 10**6),
    )(*args)


def size(axis):
    return math.prod(lax.axis_size(a) for a in axis) if isinstance(axis, tuple) else lax.axis_size(axis)


def shifted(value, axis, steps):
    count = size(axis)
    initial, last = (max(0, -steps), min(count, count - steps))
    return lax.ppermute(value, axis, [(source, source + steps) for source in range(initial, last)])


def layer(feats, cotangent, w_value, w_logit, w_out, row_offsets, col_offsets, fractions, present):
    inputs = feats.reshape(CELLS, C)
    grad_out = cotangent.reshape(CELLS, C)
    count = size(TM)
    cots = [None] * K
    cots[1] = shifted(grad_out, TM, -2)
    cots[4] = shifted(grad_out, TM, -16)
    near = lax.ppermute(grad_out, TM, [(i, i - 1) for i in range(1, count, 2)])
    cots[3] = shifted(grad_out, TM, -8)
    values, attn, packets, d0, accum, gwo, wl_t = prep(
        present, inputs, grad_out, w_value, w_logit.T, w_out, row_offsets[0], col_offsets[0], fractions[0]
    )
    cots[2] = shifted(cots[1], TM, -2)
    far = lax.ppermute(cots[1], TM, [(i, i + 1) for i in range(0, count, 2)])
    cots[0] = near + far
    packs = [None] * K
    for k in SLOTS:
        packs[k] = shifted(packets[k], TM, -DISTANCES[k])
    low = shifted(values[CELLS - COLS :], "band", 1)
    high = shifted(values[:COLS], "band", -1)
    ext = jnp.concatenate([low, values, high], axis=0)
    grads = [None] * K
    back = [None] * K
    for k in SLOTS:
        grads[k], accum, gwo = slot_call(cots[k], packs[k], ext, w_out, accum, gwo)
        back[k] = shifted(grads[k], TM, DISTANCES[k])
    from_next = shifted(accum[:COLS].astype(BF16), "band", -1)
    from_prev = shifted(accum[EXT - COLS :].astype(BF16), "band", 1)
    grad_feats, keep, send = final(
        inputs, grad_out, w_value, wl_t, attn, d0, *back, accum, from_prev, from_next, gwo
    )
    swap = [(0, 1), (1, 0)]
    both = ("pair", "band")
    count = size(both)
    share = C // count
    part = keep + lax.ppermute(send, "core", swap)
    pieces = lax.all_to_all(part, both, 0, 0, tiled=True)
    mine = jnp.sum(pieces.reshape(count, share, PAY), axis=0)
    spread = jnp.broadcast_to(mine[None], (count, share, PAY)).reshape(C, PAY)
    own = lax.all_to_all(spread, both, 0, 0, tiled=True)
    other = lax.ppermute(own, "core", swap)
    first = lax.axis_index("core") == 0
    upper = jnp.where(first, own, other)
    lower = jnp.where(first, other, own)
    half = H * J // 2
    gwl = jnp.concatenate([upper[:, C : C + half], lower[:, C : C + half]], axis=1)
    return (grad_feats.reshape(feats.shape), lower[:, :C], gwl, upper[:, :C])


def solution(mesh):
    frames, bands = mesh.shape["tm"], mesh.shape["band"]
    inner = jax.sharding.Mesh(
        np.asarray(mesh.devices).reshape(frames // 2, 2, bands), ("pair", "core", "band")
    )
    placed = (
        P(TM, "band", None, None),
        P(TM, "band", None, None),
        P(),
        P(),
        P(),
        P(TM, None, "band", None),
        P(TM, None, "band", None),
        P(TM, None, None, "band", None),
        P(TM, None),
    )
    return jax.shard_map(
        layer,
        mesh=inner,
        in_specs=placed,
        out_specs=(P(TM, "band", None, None), P(), P(), P()),
        check_vma=False,
    )
```

```python
import functools
import math

import jax
import numpy as np
import jax.numpy as jnp
from jax import lax
from jax.experimental import pallas as pl
from jax.experimental.pallas import tpu as pltpu
from jax.sharding import PartitionSpec as P


H = 8
E = 32
K = 5
J = 6
C = 256
COLS = 128
ROWS = 8
CELLS = ROWS * COLS
EXT = CELLS + 2 * COLS
PAY = 384
PACK = 64
DISTANCES = (1, 2, 4, 8, 16)
SLOTS = (4, 1, 0, 2, 3)

TM = ("pair", "core")

F32 = jnp.float32
BF16 = jnp.bfloat16


def mm(a, b, ca, cb):
    return lax.dot_general(a, b, (((ca,), (cb,)), ((), ())), preferred_element_type=F32)


def iota(shape, dim):
    return lax.broadcasted_iota(jnp.int32, shape, dim)


def head_spread():
    return jnp.where(iota((H, C), 1) // E == iota((H, C), 0), 1.0, 0.0).astype(BF16)


def head_sums(spread, prod):
    high = prod.astype(BF16)
    low = (prod - high.astype(F32)).astype(BF16)
    return mm(spread, high, 1, 1) + mm(spread, low, 1, 1)


def rows_of(r):
    return pl.ds(r * COLS, COLS)


def prep_body(
    present, feats_hbm, cot_hbm, w_value_hbm, w_logit_hbm, w_out_hbm, row_hbm, col_hbm, fracs_hbm,
    values, attn, m16, m2, m1, m8, dattn, accum, gwo, wl_t,
    mix, feats, cot, w_value, w_logit, w_out, row_off, col_off, fracs, sems,
):
    frame = lax.axis_index(TM)
    moves = (
        (w_logit_hbm, w_logit), (w_value_hbm, w_value), (feats_hbm, feats), (row_hbm, row_off),
        (col_hbm, col_off), (fracs_hbm, fracs), (w_out_hbm, w_out), (cot_hbm, cot),
    )
    copies = [pltpu.make_async_copy(src, dst, sems.at[i]) for i, (src, dst) in enumerate(moves)]
    for copy in copies:
        copy.start()
    for copy in copies:
        copy.wait()
    r48 = iota((H * J, H * J), 0)
    c48 = iota((H * J, H * J), 1)
    order = jnp.where(c48 == (r48 % H) * J + r48 // H, 1.0, 0.0).astype(BF16)
    wl = mm(order, w_logit[...], 1, 0).astype(BF16)
    wl_t[...] = wl
    spread = head_spread()
    places = (
        ((m1, CELLS), (m2, PACK + CELLS)),
        ((m2, 2 * PACK + CELLS),),
        ((m2, 0),),
        ((m8, CELLS),),
        ((m16, CELLS),),
    )
    for message, start in ((m16, 0), (m2, PACK), (m1, 0), (m8, 0)):
        message[pl.ds(start, CELLS), :] = cot[...]
    valid = [None]
    for k in range(K):
        valid.append((present[0, k] == 1) & (frame >= DISTANCES[k]))
    accum[pl.ds(0, COLS), :] = jnp.zeros((COLS, C), F32)
    accum[pl.ds(EXT - COLS, COLS), :] = jnp.zeros((COLS, C), F32)
    for r in range(ROWS):
        f = feats[rows_of(r), :]
        v = mm(f, w_value[...], 1, 0).astype(BF16)
        values[rows_of(r), :] = v
        logits = mm(wl, f, 1, 1)
        masked = [logits[0:H]]
        for k in range(K):
            part = logits[(k + 1) * H : (k + 2) * H]
            masked.append(jnp.where(valid[k + 1], part, -1e30))
        top = masked[0]
        for part in masked[1:]:
            top = jnp.maximum(top, part)
        expo = [jnp.exp(masked[0] - top)]
        for k in range(K):
            expo.append(jnp.where(valid[k + 1], jnp.exp(masked[k + 1] - top), 0.0))
        total = expo[0]
        for part in expo[1:]:
            total = total + part
        weights = [part / total for part in expo]
        attn[:, rows_of(r)] = jnp.concatenate(weights, axis=0)
        for k in range(K):
            head = jnp.concatenate(
                [
                    weights[k + 1],
                    col_off[k, r : r + 1, :].astype(F32),
                    row_off[k, r : r + 1, :].astype(F32),
                    fracs[0, k, r : r + 1, :].astype(F32),
                    fracs[1, k, r : r + 1, :].astype(F32),
                    jnp.zeros((4, COLS), F32),
                ],
                axis=0,
            )
            pack = head.astype(BF16)
            for message, start in places[k]:
                message[pl.ds(start + 16 * (r // 2), 16), pl.ds((r % 2) * COLS, COLS)] = pack
        wide = mm(weights[0].astype(BF16), spread, 0, 0)
        dm = mm(cot[rows_of(r), :], w_out[...], 1, 1).astype(BF16).astype(F32)
        vf = v.astype(F32)
        dattn[:, rows_of(r)] = head_sums(spread, dm * vf)
        accum[rows_of(r + 1), :] = (wide * dm).astype(BF16).astype(F32)
        mix[rows_of(r), :] = (wide * vf).astype(BF16)
    gwo[...] = mm(mix[...], cot[...], 0, 0)


def ext_body(values, low, high, w_value, ext):
    ext[pl.ds(0, COLS), :] = mm(low[...], w_value[...], 1, 0).astype(BF16)
    ext[pl.ds(COLS, CELLS), :] = values[...]
    ext[pl.ds(COLS + CELLS, COLS), :] = mm(high[...], w_value[...], 1, 0).astype(BF16)


def slot_body(
    cot_at, pack_at, message, ext, w_out, accum_in, gwo_in, dattn, accum, gwo, mix
):
    spread = head_spread()
    src = iota((COLS, COLS), 0).astype(F32)
    lane = iota((1, COLS), 1).astype(F32)
    accum[...] = accum_in[...]
    for r in range(ROWS):
        pack = message[pl.ds(pack_at + 16 * (r // 2), 16), pl.ds((r % 2) * COLS, COLS)]
        info = pack[8:16].astype(F32)
        c0 = lane + info[0:1]
        up = info[1:2] < -0.5
        a = info[2:3] * (1.0 / 64.0)
        b = info[3:4]
        near = 0.125 - a
        columns = jnp.where(src == c0, 8.0 - b, 0.0) + jnp.where(src == c0 + 1.0, b, 0.0)
        w0 = jnp.where(up, near, 0.0)
        w1 = jnp.where(up, a, near)
        w2 = jnp.where(up, 0.0, a)
        table = jnp.concatenate(
            [(columns * w0).astype(BF16), (columns * w1).astype(BF16), (columns * w2).astype(BF16)],
            axis=0,
        )
        window = pl.ds(r * COLS, 3 * COLS)
        taken = mm(table, ext[window, :], 0, 0).astype(BF16).astype(F32)
        wide = mm(pack[0:H], spread, 0, 0)
        cot = message[pl.ds(cot_at + r * COLS, COLS), :]
        dm = mm(cot, w_out[...], 1, 1).astype(BF16).astype(F32)
        dattn[:, rows_of(r)] = head_sums(spread, dm * taken)
        mix[rows_of(r), :] = (wide * taken).astype(BF16)
        accum[window, :] += mm(table, (wide * dm).astype(BF16), 1, 0)
    gwo[...] = gwo_in[...] + mm(mix[...], message[pl.ds(cot_at, CELLS), :], 0, 0)


def value_body(feats, low, high, accum, gwo, keep, send, dv):
    dv[...] = accum[...].astype(BF16)
    gwv = mm(feats[...], dv[pl.ds(COLS, CELLS), :], 0, 0)
    gwv = gwv + mm(low[...], dv[pl.ds(0, COLS), :], 0, 0)
    gwv = gwv + mm(high[...], dv[pl.ds(COLS + CELLS, COLS), :], 0, 0)
    core = lax.axis_index("core")
    for mine in (0, 1):

        @pl.when(core == mine)
        def _():
            keep[...] = gwo[...] if mine == 0 else gwv
            send[...] = gwv if mine == 0 else gwo[...]


def logit_body(feats, attn, d0, d1, d2, d3, d4, d5, keep, came, dl_t, pay, dl):
    grads = (d0, d1, d2, d3, d4, d5)
    r48 = iota((H * J, COLS), 0)
    c48 = iota((H * J, COLS), 1)
    order = jnp.where(c48 == (r48 % H) * J + r48 // H, 1.0, 0.0).astype(BF16)
    weights = [attn[pl.ds(j * H, H), :] for j in range(J)]
    terms = [grads[j][...] for j in range(J)]
    mean = weights[0] * terms[0]
    for j in range(1, J):
        mean = mean + weights[j] * terms[j]
    low = jnp.concatenate(
        [weights[j] * (terms[j] - mean) for j in range(J)], axis=0
    ).astype(BF16)
    dl_t[...] = low
    for r in range(ROWS):
        dl[rows_of(r), :] = mm(low[:, r * COLS : (r + 1) * COLS], order, 0, 0).astype(BF16)
    pay[:, pl.ds(0, C)] = keep[...] + came[...]
    pay[:, pl.ds(C, COLS)] = mm(feats[...], dl[...], 0, 0)


def feats_body(cot, w_value, wl_t, dl_t, accum, from_prev, from_next, grad_feats):
    for r in range(ROWS):
        center = accum[rows_of(r + 1), :]
        if r == 0:
            center = center + from_prev[...].astype(F32)
        if r == ROWS - 1:
            center = center + from_next[...].astype(F32)
        out = cot[rows_of(r), :].astype(F32) + mm(center.astype(BF16), w_value[...], 1, 1)
        out = out + mm(dl_t[:, rows_of(r)], wl_t[...], 0, 0)
        grad_feats[rows_of(r), :] = out.astype(BF16)


VM = pl.BlockSpec(memory_space=pltpu.VMEM)
SM = pl.BlockSpec(memory_space=pltpu.SMEM)
HB = pl.BlockSpec(memory_space=pltpu.HBM)


def sds(shape, dtype):
    return jax.ShapeDtypeStruct(shape, dtype)


def cost(flops, nbytes):
    return pl.CostEstimate(flops=flops, bytes_accessed=nbytes, transcendentals=0)


PARAMS = pltpu.CompilerParams(vmem_limit_bytes=48 * 1024 * 1024)


def prep(present, feats, cot, w_value, w_logit, w_out, row_off, col_off, fracs):
    return pl.pallas_call(
        prep_body,
        name="prep",
        out_shape=(
            sds((CELLS, C), BF16),
            sds((H * J, CELLS), F32),
            sds((CELLS + PACK, C), BF16),
            sds((CELLS + 3 * PACK, C), BF16),
            sds((CELLS + PACK, C), BF16),
            sds((CELLS + PACK, C), BF16),
            sds((H, CELLS), F32),
            sds((EXT, C), F32),
            sds((C, C), F32),
            sds((H * J, C), BF16),
        ),
        in_specs=[SM] + [HB] * 8,
        out_specs=(VM,) * 10,
        scratch_shapes=[
            pltpu.VMEM((CELLS, C), BF16),
            pltpu.VMEM((CELLS, C), BF16),
            pltpu.VMEM((CELLS, C), BF16),
            pltpu.VMEM((C, C), BF16),
            pltpu.VMEM((H * J, C), BF16),
            pltpu.VMEM((C, C), BF16),
            pltpu.VMEM((K, ROWS, COLS), jnp.int32),
            pltpu.VMEM((K, ROWS, COLS), jnp.int32),
            pltpu.VMEM((2, K, ROWS, COLS), jnp.int32),
            pltpu.SemaphoreType.DMA((8,)),
        ],
        compiler_params=PARAMS,
        cost_estimate=cost(10**9, 4 * 10**6),
    )(
        present,
        *(
            pltpu.with_memory_space_constraint(x, pltpu.HBM)
            for x in (feats, cot, w_value, w_logit, w_out, row_off, col_off, fracs)
        ),
    )


def slot_call(cot_at, pack_at, message, ext, w_out, accum, gwo):
    return pl.pallas_call(
        functools.partial(slot_body, cot_at, pack_at),
        name="slot",
        out_shape=(sds((H, CELLS), F32), sds((EXT, C), F32), sds((C, C), F32)),
        in_specs=[VM] * 5,
        out_specs=(VM,) * 3,
        scratch_shapes=[pltpu.VMEM((CELLS, C), BF16)],
        input_output_aliases={3: 1, 4: 2},
        compiler_params=PARAMS,
        cost_estimate=cost(10**9, 4 * 10**6),
    )(message, ext, w_out, accum, gwo)


def plain(body, outs, scratch, *args):
    return pl.pallas_call(
        body,
        out_shape=outs,
        in_specs=[VM] * len(args),
        out_specs=(VM,) * len(outs),
        scratch_shapes=scratch,
        compiler_params=PARAMS,
        cost_estimate=cost(2 * 10**8, 2 * 10**6),
    )(*args)


def size(axis):
    return math.prod(lax.axis_size(a) for a in axis) if isinstance(axis, tuple) else lax.axis_size(axis)


def shifted(value, axis, steps):
    count = size(axis)
    initial, last = (max(0, -steps), min(count, count - steps))
    return lax.ppermute(value, axis, [(source, source + steps) for source in range(initial, last)])


def layer(feats, cotangent, w_value, w_logit, w_out, row_offsets, col_offsets, fractions, present):
    inputs = feats.reshape(CELLS, C)
    grad_out = cotangent.reshape(CELLS, C)
    count = size(TM)
    low = shifted(inputs[CELLS - COLS :], "band", 1)
    high = shifted(inputs[:COLS], "band", -1)
    values, attn, m16, m2, m1, m8, d0, accum, gwo, wl_t = prep(
        present, inputs, grad_out, w_value, w_logit.T, w_out, row_offsets[0], col_offsets[0], fractions[0]
    )
    messages = [None] * K
    messages[1] = shifted(m2, TM, -2)
    messages[4] = shifted(m16, TM, -16)
    messages[3] = shifted(m8, TM, -8)
    near = lax.ppermute(m1, TM, [(i, i - 1) for i in range(1, count, 2)])
    (ext,) = plain(ext_body, (sds((EXT, C), BF16),), [], values, low, high, w_value)
    messages[2] = shifted(messages[1][: CELLS + PACK], TM, -2)
    far = lax.ppermute(
        messages[1][PACK : CELLS + 2 * PACK], TM, [(i, i + 1) for i in range(0, count, 2)]
    )
    messages[0] = near + far
    places = ((0, CELLS), (PACK, CELLS + 2 * PACK), (PACK, 0), (0, CELLS), (0, CELLS))
    grads = [None] * K
    back = [None] * K
    for k in SLOTS:
        grads[k], accum, gwo = slot_call(*places[k], messages[k], ext, w_out, accum, gwo)
        back[k] = shifted(grads[k], TM, DISTANCES[k])
    swap = [(0, 1), (1, 0)]
    square = sds((C, C), F32)
    keep, send = plain(
        value_body, (square, square), [pltpu.VMEM((EXT, C), BF16)],
        inputs, low, high, accum, gwo,
    )
    came = lax.ppermute(send, "core", swap)
    dl_t, pay = plain(
        logit_body, (sds((H * J, CELLS), BF16), sds((C, PAY), F32)),
        [pltpu.VMEM((CELLS, COLS), BF16)],
        inputs, attn, d0, *back, keep, came,
    )
    both = ("pair", "band")
    count = size(both)
    share = C // count
    pieces = lax.all_to_all(pay, both, 0, 0, tiled=True)
    from_next = shifted(accum[:COLS].astype(BF16), "band", -1)
    from_prev = shifted(accum[EXT - COLS :].astype(BF16), "band", 1)
    mine = jnp.sum(pieces.reshape(count, share, PAY), axis=0)
    spread = jnp.broadcast_to(mine[None], (count, share, PAY)).reshape(C, PAY)
    own = lax.all_to_all(spread, both, 0, 0, tiled=True)
    (grad_feats,) = plain(
        feats_body, (sds((CELLS, C), BF16),), [],
        grad_out, w_value, wl_t, dl_t, accum, from_prev, from_next,
    )
    other = lax.ppermute(own, "core", swap)
    first = lax.axis_index("core") == 0
    own_square, other_square = own[:, :C], other[:, :C]
    gwl = (own[:, C:] + other[:, C:])[:, : H * J]
    return (
        grad_feats.reshape(feats.shape),
        jnp.where(first, other_square, own_square),
        gwl,
        jnp.where(first, own_square, other_square),
    )


def solution(mesh):
    frames, bands = mesh.shape["tm"], mesh.shape["band"]
    inner = jax.sharding.Mesh(
        np.asarray(mesh.devices).reshape(frames // 2, 2, bands), ("pair", "core", "band")
    )
    placed = (
        P(TM, "band", None, None),
        P(TM, "band", None, None),
        P(),
        P(),
        P(),
        P(TM, None, "band", None),
        P(TM, None, "band", None),
        P(TM, None, None, "band", None),
        P(TM, None),
    )
    return jax.shard_map(
        layer,
        mesh=inner,
        in_specs=placed,
        out_specs=(P(TM, "band", None, None), P(), P(), P()),
        check_vma=False,
    )
```

```python
import functools
import math

import jax
import numpy as np
import jax.numpy as jnp
from jax import lax
from jax.experimental import pallas as pl
from jax.experimental.pallas import tpu as pltpu
from jax.sharding import PartitionSpec as P


H = 8
E = 32
K = 5
J = 6
C = 256
COLS = 128
ROWS = 8
CELLS = ROWS * COLS
EXT = CELLS + 2 * COLS
PAY = 384
PACK = 64
DISTANCES = (1, 2, 4, 8, 16)
SLOTS = (4, 1, 0, 2, 3)

TM = ("pair", "core")

F32 = jnp.float32
BF16 = jnp.bfloat16


def mm(a, b, ca, cb):
    return lax.dot_general(a, b, (((ca,), (cb,)), ((), ())), preferred_element_type=F32)


def iota(shape, dim):
    return lax.broadcasted_iota(jnp.int32, shape, dim)


def head_spread():
    return jnp.where(iota((H, C), 1) // E == iota((H, C), 0), 1.0, 0.0).astype(BF16)


def head_sums(spread, prod):
    high = prod.astype(BF16)
    low = (prod - high.astype(F32)).astype(BF16)
    return mm(spread, high, 1, 1) + mm(spread, low, 1, 1)


def rows_of(r):
    return pl.ds(r * COLS, COLS)


def prep_body(
    present, feats_hbm, cot_hbm, w_value_hbm, w_logit_hbm, w_out_hbm, row_hbm, col_hbm, fracs_hbm,
    values, attn, m16, m2, m1, m8, dattn, accum, gwo, wl_t,
    mix, feats, cot, w_value, w_logit, w_out, row_off, col_off, fracs, sems,
):
    frame = lax.axis_index(TM)
    moves = (
        (w_logit_hbm, w_logit), (w_value_hbm, w_value), (feats_hbm, feats), (row_hbm, row_off),
        (col_hbm, col_off), (fracs_hbm, fracs), (w_out_hbm, w_out), (cot_hbm, cot),
    )
    copies = [pltpu.make_async_copy(src, dst, sems.at[i]) for i, (src, dst) in enumerate(moves)]
    for copy in copies:
        copy.start()
    for copy in copies:
        copy.wait()
    r48 = iota((H * J, H * J), 0)
    c48 = iota((H * J, H * J), 1)
    order = jnp.where(c48 == (r48 % H) * J + r48 // H, 1.0, 0.0).astype(BF16)
    wl = mm(order, w_logit[...], 1, 0).astype(BF16)
    wl_t[...] = wl
    spread = head_spread()
    places = (
        ((m1, CELLS), (m2, PACK + CELLS)),
        ((m2, 2 * PACK + CELLS),),
        ((m2, 0),),
        ((m8, CELLS),),
        ((m16, CELLS),),
    )
    for message, start in ((m16, 0), (m2, PACK), (m1, 0), (m8, 0)):
        message[pl.ds(start, CELLS), :] = cot[...]
    valid = [None]
    for k in range(K):
        valid.append((present[0, k] == 1) & (frame >= DISTANCES[k]))
    accum[pl.ds(0, COLS), :] = jnp.zeros((COLS, C), F32)
    accum[pl.ds(EXT - COLS, COLS), :] = jnp.zeros((COLS, C), F32)
    for r in range(ROWS):
        f = feats[rows_of(r), :]
        v = mm(f, w_value[...], 1, 0).astype(BF16)
        values[rows_of(r), :] = v
        logits = mm(wl, f, 1, 1)
        masked = [logits[0:H]]
        for k in range(K):
            part = logits[(k + 1) * H : (k + 2) * H]
            masked.append(jnp.where(valid[k + 1], part, -1e30))
        top = masked[0]
        for part in masked[1:]:
            top = jnp.maximum(top, part)
        expo = [jnp.exp(masked[0] - top)]
        for k in range(K):
            expo.append(jnp.where(valid[k + 1], jnp.exp(masked[k + 1] - top), 0.0))
        total = expo[0]
        for part in expo[1:]:
            total = total + part
        weights = [part / total for part in expo]
        attn[:, rows_of(r)] = jnp.concatenate(weights, axis=0)
        for k in range(K):
            head = jnp.concatenate(
                [
                    weights[k + 1],
                    col_off[k, r : r + 1, :].astype(F32),
                    row_off[k, r : r + 1, :].astype(F32),
                    fracs[0, k, r : r + 1, :].astype(F32),
                    fracs[1, k, r : r + 1, :].astype(F32),
                    jnp.zeros((4, COLS), F32),
                ],
                axis=0,
            )
            pack = head.astype(BF16)
            for message, start in places[k]:
                message[pl.ds(start + 16 * (r // 2), 16), pl.ds((r % 2) * COLS, COLS)] = pack
        wide = mm(weights[0].astype(BF16), spread, 0, 0)
        dm = mm(cot[rows_of(r), :], w_out[...], 1, 1).astype(BF16).astype(F32)
        vf = v.astype(F32)
        dattn[:, rows_of(r)] = head_sums(spread, dm * vf)
        accum[rows_of(r + 1), :] = (wide * dm).astype(BF16).astype(F32)
        mix[rows_of(r), :] = (wide * vf).astype(BF16)
    gwo[...] = mm(mix[...], cot[...], 0, 0)


def ext_body(values, low, high, w_value, ext):
    ext[pl.ds(0, COLS), :] = mm(low[...], w_value[...], 1, 0).astype(BF16)
    ext[pl.ds(COLS, CELLS), :] = values[...]
    ext[pl.ds(COLS + CELLS, COLS), :] = mm(high[...], w_value[...], 1, 0).astype(BF16)


def slot_body(
    cot_at, pack_at, message, ext, w_out, accum_in, gwo_in, dattn, accum, gwo, mix
):
    spread = head_spread()
    src = iota((COLS, COLS), 0).astype(F32)
    lane = iota((1, COLS), 1).astype(F32)
    accum[...] = accum_in[...]
    for r in range(ROWS):
        pack = message[pl.ds(pack_at + 16 * (r // 2), 16), pl.ds((r % 2) * COLS, COLS)]
        info = pack[8:16].astype(F32)
        c0 = lane + info[0:1]
        up = info[1:2] < -0.5
        a = info[2:3] * (1.0 / 64.0)
        b = info[3:4]
        near = 0.125 - a
        columns = jnp.where(src == c0, 8.0 - b, 0.0) + jnp.where(src == c0 + 1.0, b, 0.0)
        w0 = jnp.where(up, near, 0.0)
        w1 = jnp.where(up, a, near)
        w2 = jnp.where(up, 0.0, a)
        table = jnp.concatenate(
            [(columns * w0).astype(BF16), (columns * w1).astype(BF16), (columns * w2).astype(BF16)],
            axis=0,
        )
        window = pl.ds(r * COLS, 3 * COLS)
        taken = mm(table, ext[window, :], 0, 0).astype(BF16).astype(F32)
        wide = mm(pack[0:H], spread, 0, 0)
        cot = message[pl.ds(cot_at + r * COLS, COLS), :]
        dm = mm(cot, w_out[...], 1, 1).astype(BF16).astype(F32)
        dattn[:, rows_of(r)] = head_sums(spread, dm * taken)
        mix[rows_of(r), :] = (wide * taken).astype(BF16)
        accum[window, :] += mm(table, (wide * dm).astype(BF16), 1, 0)
    gwo[...] = gwo_in[...] + mm(mix[...], message[pl.ds(cot_at, CELLS), :], 0, 0)


def value_body(feats, low, high, accum, gwo, keep, send, rim_low, rim_high, dv):
    dv[...] = accum[...].astype(BF16)
    gwv = mm(feats[...], dv[pl.ds(COLS, CELLS), :], 0, 0)
    gwv = gwv + mm(low[...], dv[pl.ds(0, COLS), :], 0, 0)
    gwv = gwv + mm(high[...], dv[pl.ds(COLS + CELLS, COLS), :], 0, 0)
    rim_low[...] = dv[pl.ds(0, COLS), :]
    rim_high[...] = dv[pl.ds(COLS + CELLS, COLS), :]
    core = lax.axis_index("core")
    for mine in (0, 1):

        @pl.when(core == mine)
        def _():
            keep[...] = gwo[...] if mine == 0 else gwv
            send[...] = gwv if mine == 0 else gwo[...]


def logit_body(feats, attn, d0, d1, d2, d3, d4, d5, keep, came, dl_t, pay, dl):
    grads = (d0, d1, d2, d3, d4, d5)
    r48 = iota((H * J, COLS), 0)
    c48 = iota((H * J, COLS), 1)
    order = jnp.where(c48 == (r48 % H) * J + r48 // H, 1.0, 0.0).astype(BF16)
    weights = [attn[pl.ds(j * H, H), :] for j in range(J)]
    terms = [grads[j][...] for j in range(J)]
    mean = weights[0] * terms[0]
    for j in range(1, J):
        mean = mean + weights[j] * terms[j]
    low = jnp.concatenate(
        [weights[j] * (terms[j] - mean) for j in range(J)], axis=0
    ).astype(BF16)
    dl_t[...] = low
    for r in range(ROWS):
        dl[rows_of(r), :] = mm(low[:, r * COLS : (r + 1) * COLS], order, 0, 0).astype(BF16)
    pay[:, pl.ds(0, C)] = keep[...] + came[...]
    pay[:, pl.ds(C, COLS)] = mm(feats[...], dl[...], 0, 0)


def feats_body(cot, w_value, wl_t, dl_t, accum, from_prev, from_next, grad_feats):
    for r in range(ROWS):
        center = accum[rows_of(r + 1), :]
        if r == 0:
            center = center + from_prev[...].astype(F32)
        if r == ROWS - 1:
            center = center + from_next[...].astype(F32)
        out = cot[rows_of(r), :].astype(F32) + mm(center.astype(BF16), w_value[...], 1, 1)
        out = out + mm(dl_t[:, rows_of(r)], wl_t[...], 0, 0)
        grad_feats[rows_of(r), :] = out.astype(BF16)


VM = pl.BlockSpec(memory_space=pltpu.VMEM)
SM = pl.BlockSpec(memory_space=pltpu.SMEM)
HB = pl.BlockSpec(memory_space=pltpu.HBM)


def sds(shape, dtype):
    return jax.ShapeDtypeStruct(shape, dtype)


def cost(flops, nbytes):
    return pl.CostEstimate(flops=flops, bytes_accessed=nbytes, transcendentals=0)


PARAMS = pltpu.CompilerParams(vmem_limit_bytes=48 * 1024 * 1024)


def prep(present, feats, cot, w_value, w_logit, w_out, row_off, col_off, fracs):
    return pl.pallas_call(
        prep_body,
        name="prep",
        out_shape=(
            sds((CELLS, C), BF16),
            sds((H * J, CELLS), F32),
            sds((CELLS + PACK, C), BF16),
            sds((CELLS + 3 * PACK, C), BF16),
            sds((CELLS + PACK, C), BF16),
            sds((CELLS + PACK, C), BF16),
            sds((H, CELLS), F32),
            sds((EXT, C), F32),
            sds((C, C), F32),
            sds((H * J, C), BF16),
        ),
        in_specs=[SM] + [HB] * 8,
        out_specs=(VM,) * 10,
        scratch_shapes=[
            pltpu.VMEM((CELLS, C), BF16),
            pltpu.VMEM((CELLS, C), BF16),
            pltpu.VMEM((CELLS, C), BF16),
            pltpu.VMEM((C, C), BF16),
            pltpu.VMEM((H * J, C), BF16),
            pltpu.VMEM((C, C), BF16),
            pltpu.VMEM((K, ROWS, COLS), jnp.int32),
            pltpu.VMEM((K, ROWS, COLS), jnp.int32),
            pltpu.VMEM((2, K, ROWS, COLS), jnp.int32),
            pltpu.SemaphoreType.DMA((8,)),
        ],
        compiler_params=PARAMS,
        cost_estimate=cost(10**9, 4 * 10**6),
    )(
        present,
        *(
            pltpu.with_memory_space_constraint(x, pltpu.HBM)
            for x in (feats, cot, w_value, w_logit, w_out, row_off, col_off, fracs)
        ),
    )


def slot_call(cot_at, pack_at, message, ext, w_out, accum, gwo):
    return pl.pallas_call(
        functools.partial(slot_body, cot_at, pack_at),
        name="slot",
        out_shape=(sds((H, CELLS), F32), sds((EXT, C), F32), sds((C, C), F32)),
        in_specs=[VM] * 5,
        out_specs=(VM,) * 3,
        scratch_shapes=[pltpu.VMEM((CELLS, C), BF16)],
        input_output_aliases={3: 1, 4: 2},
        compiler_params=PARAMS,
        cost_estimate=cost(10**9, 4 * 10**6),
    )(message, ext, w_out, accum, gwo)


def plain(body, outs, scratch, *args):
    return pl.pallas_call(
        body,
        out_shape=outs,
        in_specs=[VM] * len(args),
        out_specs=(VM,) * len(outs),
        scratch_shapes=scratch,
        compiler_params=PARAMS,
        cost_estimate=cost(2 * 10**8, 2 * 10**6),
    )(*args)


def size(axis):
    return math.prod(lax.axis_size(a) for a in axis) if isinstance(axis, tuple) else lax.axis_size(axis)


def shifted(value, axis, steps):
    count = size(axis)
    initial, last = (max(0, -steps), min(count, count - steps))
    return lax.ppermute(value, axis, [(source, source + steps) for source in range(initial, last)])


def layer(feats, cotangent, w_value, w_logit, w_out, row_offsets, col_offsets, fractions, present):
    inputs = feats.reshape(CELLS, C)
    grad_out = cotangent.reshape(CELLS, C)
    count = size(TM)
    low = shifted(inputs[CELLS - COLS :], "band", 1)
    high = shifted(inputs[:COLS], "band", -1)
    values, attn, m16, m2, m1, m8, d0, accum, gwo, wl_t = prep(
        present, inputs, grad_out, w_value, w_logit.T, w_out, row_offsets[0], col_offsets[0], fractions[0]
    )
    messages = [None] * K
    messages[1] = shifted(m2, TM, -2)
    messages[4] = shifted(m16, TM, -16)
    messages[3] = shifted(m8, TM, -8)
    near = lax.ppermute(m1, TM, [(i, i - 1) for i in range(1, count, 2)])
    (ext,) = plain(ext_body, (sds((EXT, C), BF16),), [], values, low, high, w_value)
    messages[2] = shifted(messages[1][: CELLS + PACK], TM, -2)
    far = lax.ppermute(
        messages[1][PACK : CELLS + 2 * PACK], TM, [(i, i + 1) for i in range(0, count, 2)]
    )
    messages[0] = near + far
    places = ((0, CELLS), (PACK, CELLS + 2 * PACK), (PACK, 0), (0, CELLS), (0, CELLS))
    grads = [None] * K
    back = [None] * K
    for k in SLOTS:
        grads[k], accum, gwo = slot_call(*places[k], messages[k], ext, w_out, accum, gwo)
        back[k] = shifted(grads[k], TM, DISTANCES[k])
    swap = [(0, 1), (1, 0)]
    square = sds((C, C), F32)
    rim = sds((COLS, C), BF16)
    keep, send, rim_low, rim_high = plain(
        value_body, (square, square, rim, rim), [pltpu.VMEM((EXT, C), BF16)],
        inputs, low, high, accum, gwo,
    )
    came = lax.ppermute(send, "core", swap)
    dl_t, pay = plain(
        logit_body, (sds((H * J, CELLS), BF16), sds((C, PAY), F32)),
        [pltpu.VMEM((CELLS, COLS), BF16)],
        inputs, attn, d0, *back, keep, came,
    )
    both = ("pair", "band")
    count = size(both)
    share = C // count
    pieces = lax.all_to_all(pay, both, 0, 0, tiled=True)
    from_next = shifted(rim_low, "band", -1)
    from_prev = shifted(rim_high, "band", 1)
    mine = jnp.sum(pieces.reshape(count, share, PAY), axis=0)
    spread = jnp.broadcast_to(mine[None], (count, share, PAY)).reshape(C, PAY)
    own = lax.all_to_all(spread, both, 0, 0, tiled=True)
    (grad_feats,) = plain(
        feats_body, (sds((CELLS, C), BF16),), [],
        grad_out, w_value, wl_t, dl_t, accum, from_prev, from_next,
    )
    other = lax.ppermute(own, "core", swap)
    first = lax.axis_index("core") == 0
    own_square, other_square = own[:, :C], other[:, :C]
    gwl = (own[:, C:] + other[:, C:])[:, : H * J]
    return (
        grad_feats.reshape(feats.shape),
        jnp.where(first, other_square, own_square),
        gwl,
        jnp.where(first, own_square, other_square),
    )


def solution(mesh):
    frames, bands = mesh.shape["tm"], mesh.shape["band"]
    inner = jax.sharding.Mesh(
        np.asarray(mesh.devices).reshape(frames // 2, 2, bands), ("pair", "core", "band")
    )
    placed = (
        P(TM, "band", None, None),
        P(TM, "band", None, None),
        P(),
        P(),
        P(),
        P(TM, None, "band", None),
        P(TM, None, "band", None),
        P(TM, None, None, "band", None),
        P(TM, None),
    )
    return jax.shard_map(
        layer,
        mesh=inner,
        in_specs=placed,
        out_specs=(P(TM, "band", None, None), P(), P(), P()),
        check_vma=False,
    )
```

```python
import functools
import math

import jax
import numpy as np
import jax.numpy as jnp
from jax import lax
from jax.experimental import pallas as pl
from jax.experimental.pallas import tpu as pltpu
from jax.sharding import PartitionSpec as P


H = 8
E = 32
K = 5
J = 6
C = 256
COLS = 128
ROWS = 8
CELLS = ROWS * COLS
EXT = CELLS + 2 * COLS
PAY = 384
PACK = 64
RUN = 16
DISTANCES = (1, 2, 4, 8, 16)
SLOTS = (4, 1, 0, 2, 3)

TM = ("pair", "core")

F32 = jnp.float32
BF16 = jnp.bfloat16


def mm(a, b, ca, cb):
    return lax.dot_general(a, b, (((ca,), (cb,)), ((), ())), preferred_element_type=F32)


def iota(shape, dim):
    return lax.broadcasted_iota(jnp.int32, shape, dim)


def head_spread():
    return jnp.where(iota((H, C), 1) // E == iota((H, C), 0), 1.0, 0.0).astype(BF16)


def head_sums(spread, prod):
    high = prod.astype(BF16)
    low = (prod - high.astype(F32)).astype(BF16)
    return mm(spread, high, 1, 1) + mm(spread, low, 1, 1)


def rows_of(r):
    return pl.ds(r * COLS, COLS)


def prep_body(
    present, feats_hbm, cot_hbm, w_value_hbm, w_logit_hbm, w_out_hbm, row_hbm, col_hbm, fracs_hbm,
    values, attn, m16, m2, m1, dattn, accum, gwo, wl_t,
    mix, feats, cot, w_value, w_logit, w_out, row_off, col_off, fracs, sems,
):
    frame = lax.axis_index(TM)
    moves = (
        (w_logit_hbm, w_logit), (w_value_hbm, w_value), (feats_hbm, feats), (row_hbm, row_off),
        (col_hbm, col_off), (fracs_hbm, fracs), (w_out_hbm, w_out), (cot_hbm, cot),
    )
    copies = [pltpu.make_async_copy(src, dst, sems.at[i]) for i, (src, dst) in enumerate(moves)]
    for copy in copies:
        copy.start()
    for copy in copies:
        copy.wait()
    r48 = iota((H * J, H * J), 0)
    c48 = iota((H * J, H * J), 1)
    order = jnp.where(c48 == (r48 % H) * J + r48 // H, 1.0, 0.0).astype(BF16)
    wl = mm(order, w_logit[...], 1, 0).astype(BF16)
    wl_t[...] = wl
    spread = head_spread()
    places = (
        ((m1, CELLS), (m2, PACK + CELLS)),
        ((m2, 2 * PACK + CELLS),),
        ((m2, 0),),
        ((m16, CELLS),),
        ((m16, CELLS + PACK),),
    )
    for message, start in ((m16, 0), (m2, PACK), (m1, 0)):
        message[pl.ds(start, CELLS), :] = cot[...]
    valid = [None]
    for k in range(K):
        valid.append((present[0, k] == 1) & (frame >= DISTANCES[k]))
    accum[pl.ds(0, COLS), :] = jnp.zeros((COLS, C), F32)
    accum[pl.ds(EXT - COLS, COLS), :] = jnp.zeros((COLS, C), F32)
    for r in range(ROWS):
        f = feats[rows_of(r), :]
        v = mm(f, w_value[...], 1, 0).astype(BF16)
        values[rows_of(r), :] = v
        logits = mm(wl, f, 1, 1)
        masked = [logits[0:H]]
        for k in range(K):
            part = logits[(k + 1) * H : (k + 2) * H]
            masked.append(jnp.where(valid[k + 1], part, -1e30))
        top = masked[0]
        for part in masked[1:]:
            top = jnp.maximum(top, part)
        expo = [jnp.exp(masked[0] - top)]
        for k in range(K):
            expo.append(jnp.where(valid[k + 1], jnp.exp(masked[k + 1] - top), 0.0))
        total = expo[0]
        for part in expo[1:]:
            total = total + part
        weights = [part / total for part in expo]
        attn[:, rows_of(r)] = jnp.concatenate(weights, axis=0)
        for k in range(K):
            head = jnp.concatenate(
                [
                    weights[k + 1],
                    col_off[k, r : r + 1, :].astype(F32),
                    row_off[k, r : r + 1, :].astype(F32),
                    fracs[0, k, r : r + 1, :].astype(F32),
                    fracs[1, k, r : r + 1, :].astype(F32),
                    jnp.zeros((4, COLS), F32),
                ],
                axis=0,
            )
            pack = head.astype(BF16)
            for message, start in places[k]:
                message[pl.ds(start + 16 * (r // 2), 16), pl.ds((r % 2) * COLS, COLS)] = pack
        wide = mm(weights[0].astype(BF16), spread, 0, 0)
        dm = mm(cot[rows_of(r), :], w_out[...], 1, 1).astype(BF16).astype(F32)
        vf = v.astype(F32)
        dattn[:, rows_of(r)] = head_sums(spread, dm * vf)
        accum[rows_of(r + 1), :] = (wide * dm).astype(BF16).astype(F32)
        mix[rows_of(r), :] = (wide * vf).astype(BF16)
    gwo[...] = mm(mix[...], cot[...], 0, 0)


def pick_body(came, own, out):
    early = lax.rem(lax.axis_index(TM), RUN) < RUN // 2

    @pl.when(early)
    def _():
        out[...] = came[pl.ds(0, CELLS + PACK), :]

    @pl.when(jnp.logical_not(early))
    def _():
        out[...] = own[pl.ds(0, CELLS + PACK), :]


def ext_body(values, low, high, w_value, ext):
    ext[pl.ds(0, COLS), :] = mm(low[...], w_value[...], 1, 0).astype(BF16)
    ext[pl.ds(COLS, CELLS), :] = values[...]
    ext[pl.ds(COLS + CELLS, COLS), :] = mm(high[...], w_value[...], 1, 0).astype(BF16)


def slot_body(
    cot_at, pack_at, message, ext, w_out, accum_in, gwo_in, dattn, accum, gwo, mix
):
    spread = head_spread()
    src = iota((COLS, COLS), 0).astype(F32)
    lane = iota((1, COLS), 1).astype(F32)
    accum[...] = accum_in[...]
    for r in range(ROWS):
        pack = message[pl.ds(pack_at + 16 * (r // 2), 16), pl.ds((r % 2) * COLS, COLS)]
        info = pack[8:16].astype(F32)
        c0 = lane + info[0:1]
        up = info[1:2] < -0.5
        a = info[2:3] * (1.0 / 64.0)
        b = info[3:4]
        near = 0.125 - a
        columns = jnp.where(src == c0, 8.0 - b, 0.0) + jnp.where(src == c0 + 1.0, b, 0.0)
        w0 = jnp.where(up, near, 0.0)
        w1 = jnp.where(up, a, near)
        w2 = jnp.where(up, 0.0, a)
        table = jnp.concatenate(
            [(columns * w0).astype(BF16), (columns * w1).astype(BF16), (columns * w2).astype(BF16)],
            axis=0,
        )
        window = pl.ds(r * COLS, 3 * COLS)
        taken = mm(table, ext[window, :], 0, 0).astype(BF16).astype(F32)
        wide = mm(pack[0:H], spread, 0, 0)
        cot = message[pl.ds(cot_at + r * COLS, COLS), :]
        dm = mm(cot, w_out[...], 1, 1).astype(BF16).astype(F32)
        dattn[:, rows_of(r)] = head_sums(spread, dm * taken)
        mix[rows_of(r), :] = (wide * taken).astype(BF16)
        accum[window, :] += mm(table, (wide * dm).astype(BF16), 1, 0)
    gwo[...] = gwo_in[...] + mm(mix[...], message[pl.ds(cot_at, CELLS), :], 0, 0)


def value_body(feats, low, high, accum, gwo, keep, send, rim_low, rim_high, dv):
    dv[...] = accum[...].astype(BF16)
    gwv = mm(feats[...], dv[pl.ds(COLS, CELLS), :], 0, 0)
    gwv = gwv + mm(low[...], dv[pl.ds(0, COLS), :], 0, 0)
    gwv = gwv + mm(high[...], dv[pl.ds(COLS + CELLS, COLS), :], 0, 0)
    rim_low[...] = dv[pl.ds(0, COLS), :]
    rim_high[...] = dv[pl.ds(COLS + CELLS, COLS), :]
    core = lax.axis_index("core")
    for mine in (0, 1):

        @pl.when(core == mine)
        def _():
            keep[...] = gwo[...] if mine == 0 else gwv
            send[...] = gwv if mine == 0 else gwo[...]


def logit_body(feats, attn, d0, d1, d2, d3, d4, d5, keep, came, dl_t, pay, dl):
    grads = (d0, d1, d2, d3, d4, d5)
    r48 = iota((H * J, COLS), 0)
    c48 = iota((H * J, COLS), 1)
    order = jnp.where(c48 == (r48 % H) * J + r48 // H, 1.0, 0.0).astype(BF16)
    weights = [attn[pl.ds(j * H, H), :] for j in range(J)]
    terms = [grads[j][...] for j in range(J)]
    mean = weights[0] * terms[0]
    for j in range(1, J):
        mean = mean + weights[j] * terms[j]
    low = jnp.concatenate(
        [weights[j] * (terms[j] - mean) for j in range(J)], axis=0
    ).astype(BF16)
    dl_t[...] = low
    for r in range(ROWS):
        dl[rows_of(r), :] = mm(low[:, r * COLS : (r + 1) * COLS], order, 0, 0).astype(BF16)
    pay[:, pl.ds(0, C)] = keep[...] + came[...]
    pay[:, pl.ds(C, COLS)] = mm(feats[...], dl[...], 0, 0)


def feats_body(cot, w_value, wl_t, dl_t, accum, from_prev, from_next, grad_feats):
    for r in range(ROWS):
        center = accum[rows_of(r + 1), :]
        if r == 0:
            center = center + from_prev[...].astype(F32)
        if r == ROWS - 1:
            center = center + from_next[...].astype(F32)
        out = cot[rows_of(r), :].astype(F32) + mm(center.astype(BF16), w_value[...], 1, 1)
        out = out + mm(dl_t[:, rows_of(r)], wl_t[...], 0, 0)
        grad_feats[rows_of(r), :] = out.astype(BF16)


VM = pl.BlockSpec(memory_space=pltpu.VMEM)
SM = pl.BlockSpec(memory_space=pltpu.SMEM)
HB = pl.BlockSpec(memory_space=pltpu.HBM)


def sds(shape, dtype):
    return jax.ShapeDtypeStruct(shape, dtype)


def cost(flops, nbytes):
    return pl.CostEstimate(flops=flops, bytes_accessed=nbytes, transcendentals=0)


PARAMS = pltpu.CompilerParams(vmem_limit_bytes=24 * 1024 * 1024)


def prep(present, feats, cot, w_value, w_logit, w_out, row_off, col_off, fracs):
    return pl.pallas_call(
        prep_body,
        name="prep",
        out_shape=(
            sds((CELLS, C), BF16),
            sds((H * J, CELLS), F32),
            sds((CELLS + 2 * PACK, C), BF16),
            sds((CELLS + 3 * PACK, C), BF16),
            sds((CELLS + PACK, C), BF16),
            sds((H, CELLS), F32),
            sds((EXT, C), F32),
            sds((C, C), F32),
            sds((H * J, C), BF16),
        ),
        in_specs=[SM] + [HB] * 8,
        out_specs=(VM,) * 9,
        scratch_shapes=[
            pltpu.VMEM((CELLS, C), BF16),
            pltpu.VMEM((CELLS, C), BF16),
            pltpu.VMEM((CELLS, C), BF16),
            pltpu.VMEM((C, C), BF16),
            pltpu.VMEM((H * J, C), BF16),
            pltpu.VMEM((C, C), BF16),
            pltpu.VMEM((K, ROWS, COLS), jnp.int32),
            pltpu.VMEM((K, ROWS, COLS), jnp.int32),
            pltpu.VMEM((2, K, ROWS, COLS), jnp.int32),
            pltpu.SemaphoreType.DMA((8,)),
        ],
        compiler_params=PARAMS,
        cost_estimate=cost(10**9, 4 * 10**6),
    )(
        present,
        *(
            pltpu.with_memory_space_constraint(x, pltpu.HBM)
            for x in (feats, cot, w_value, w_logit, w_out, row_off, col_off, fracs)
        ),
    )


def slot_call(cot_at, pack_at, message, ext, w_out, accum, gwo):
    return pl.pallas_call(
        functools.partial(slot_body, cot_at, pack_at),
        name="slot",
        out_shape=(sds((H, CELLS), F32), sds((EXT, C), F32), sds((C, C), F32)),
        in_specs=[VM] * 5,
        out_specs=(VM,) * 3,
        scratch_shapes=[pltpu.VMEM((CELLS, C), BF16)],
        input_output_aliases={3: 1, 4: 2},
        compiler_params=PARAMS,
        cost_estimate=cost(10**9, 4 * 10**6),
    )(message, ext, w_out, accum, gwo)


def plain(body, outs, scratch, *args):
    return pl.pallas_call(
        body,
        out_shape=outs,
        in_specs=[VM] * len(args),
        out_specs=(VM,) * len(outs),
        scratch_shapes=scratch,
        compiler_params=PARAMS,
        cost_estimate=cost(2 * 10**8, 2 * 10**6),
    )(*args)


def size(axis):
    return math.prod(lax.axis_size(a) for a in axis) if isinstance(axis, tuple) else lax.axis_size(axis)


def shifted(value, axis, steps):
    count = size(axis)
    initial, last = (max(0, -steps), min(count, count - steps))
    return lax.ppermute(value, axis, [(source, source + steps) for source in range(initial, last)])


def layer(feats, cotangent, w_value, w_logit, w_out, row_offsets, col_offsets, fractions, present):
    inputs = feats.reshape(CELLS, C)
    grad_out = cotangent.reshape(CELLS, C)
    count = size(TM)
    low = shifted(inputs[CELLS - COLS :], "band", 1)
    high = shifted(inputs[:COLS], "band", -1)
    values, attn, m16, m2, m1, d0, accum, gwo, wl_t = prep(
        present, inputs, grad_out, w_value, w_logit.T, w_out, row_offsets[0], col_offsets[0], fractions[0]
    )
    messages = [None] * K
    messages[1] = shifted(m2, TM, -2)
    messages[4] = shifted(m16, TM, -16)
    near = lax.ppermute(m1, TM, [(i, i - 1) for i in range(1, count, 2)])
    (ext,) = plain(ext_body, (sds((EXT, C), BF16),), [], values, low, high, w_value)
    messages[2] = shifted(messages[1][: CELLS + PACK], TM, -2)
    far = lax.ppermute(
        messages[1][PACK : CELLS + 2 * PACK], TM, [(i, i + 1) for i in range(0, count, 2)]
    )
    messages[0] = near + far
    if count % RUN == 0:
        (moved,) = plain(pick_body, (sds((CELLS + PACK, C), BF16),), [], messages[4], m16)
        messages[3] = lax.ppermute(
            moved, TM, [(i, i // RUN * RUN + (i + RUN // 2) % RUN) for i in range(count)]
        )
    else:
        messages[3] = shifted(m16[: CELLS + PACK], TM, -8)
    places = ((0, CELLS), (PACK, CELLS + 2 * PACK), (PACK, 0), (0, CELLS), (0, CELLS + PACK))
    grads = [None] * K
    back = [None] * K
    for k in SLOTS:
        grads[k], accum, gwo = slot_call(*places[k], messages[k], ext, w_out, accum, gwo)
        back[k] = shifted(grads[k], TM, DISTANCES[k])
    swap = [(0, 1), (1, 0)]
    square = sds((C, C), F32)
    rim = sds((COLS, C), BF16)
    keep, send, rim_low, rim_high = plain(
        value_body, (square, square, rim, rim), [pltpu.VMEM((EXT, C), BF16)],
        inputs, low, high, accum, gwo,
    )
    came = lax.ppermute(send, "core", swap)
    dl_t, pay = plain(
        logit_body, (sds((H * J, CELLS), BF16), sds((C, PAY), F32)),
        [pltpu.VMEM((CELLS, COLS), BF16)],
        inputs, attn, d0, *back, keep, came,
    )
    both = ("pair", "band")
    count = size(both)
    share = C // count
    pieces = lax.all_to_all(pay, both, 0, 0, tiled=True)
    from_next = shifted(rim_low, "band", -1)
    from_prev = shifted(rim_high, "band", 1)
    mine = jnp.sum(pieces.reshape(count, share, PAY), axis=0)
    spread = jnp.broadcast_to(mine[None], (count, share, PAY)).reshape(C, PAY)
    own = lax.all_to_all(spread, both, 0, 0, tiled=True)
    (grad_feats,) = plain(
        feats_body, (sds((CELLS, C), BF16),), [],
        grad_out, w_value, wl_t, dl_t, accum, from_prev, from_next,
    )
    other = lax.ppermute(own, "core", swap)
    first = lax.axis_index("core") == 0
    own_square, other_square = own[:, :C], other[:, :C]
    gwl = (own[:, C:] + other[:, C:])[:, : H * J]
    return (
        grad_feats.reshape(feats.shape),
        jnp.where(first, other_square, own_square),
        gwl,
        jnp.where(first, own_square, other_square),
    )


def solution(mesh):
    frames, bands = mesh.shape["tm"], mesh.shape["band"]
    inner = jax.sharding.Mesh(
        np.asarray(mesh.devices).reshape(frames // 2, 2, bands), ("pair", "core", "band")
    )
    placed = (
        P(TM, "band", None, None),
        P(TM, "band", None, None),
        P(),
        P(),
        P(),
        P(TM, None, "band", None),
        P(TM, None, "band", None),
        P(TM, None, None, "band", None),
        P(TM, None),
    )
    return jax.shard_map(
        layer,
        mesh=inner,
        in_specs=placed,
        out_specs=(P(TM, "band", None, None), P(), P(), P()),
        check_vma=False,
    )
```

```python
import functools
import math

import jax
import numpy as np
import jax.numpy as jnp
from jax import lax
from jax.experimental import pallas as pl
from jax.experimental.pallas import tpu as pltpu
from jax.sharding import PartitionSpec as P


H = 8
E = 32
K = 5
J = 6
C = 256
COLS = 128
ROWS = 8
CELLS = ROWS * COLS
EXT = CELLS + 2 * COLS
PAY = 384
PACK = 64
DISTANCES = (1, 2, 4, 8, 16)
SLOTS = (1, 0, 4, 2, 3)

TM = ("pair", "core")

F32 = jnp.float32
BF16 = jnp.bfloat16


def mm(a, b, ca, cb):
    return lax.dot_general(a, b, (((ca,), (cb,)), ((), ())), preferred_element_type=F32)


def iota(shape, dim):
    return lax.broadcasted_iota(jnp.int32, shape, dim)


def head_spread():
    return jnp.where(iota((H, C), 1) // E == iota((H, C), 0), 1.0, 0.0).astype(BF16)


def head_sums(spread, prod):
    high = prod.astype(BF16)
    low = (prod - high.astype(F32)).astype(BF16)
    return mm(spread, high, 1, 1) + mm(spread, low, 1, 1)


def rows_of(r):
    return pl.ds(r * COLS, COLS)


def prep_body(
    present, feats_hbm, cot_hbm, w_value_hbm, w_logit_hbm, w_out_hbm, row_hbm, col_hbm, fracs_hbm,
    values, attn, m16, m2, m1, dattn, accum, gwo, wl_t,
    mix, feats, cot, w_value, w_logit, w_out, row_off, col_off, fracs, sems,
):
    frame = lax.axis_index(TM)
    moves = (
        (w_logit_hbm, w_logit), (w_value_hbm, w_value), (feats_hbm, feats), (row_hbm, row_off),
        (col_hbm, col_off), (fracs_hbm, fracs), (w_out_hbm, w_out), (cot_hbm, cot),
    )
    copies = [pltpu.make_async_copy(src, dst, sems.at[i]) for i, (src, dst) in enumerate(moves)]
    for copy in copies:
        copy.start()
    for copy in copies:
        copy.wait()
    r48 = iota((H * J, H * J), 0)
    c48 = iota((H * J, H * J), 1)
    order = jnp.where(c48 == (r48 % H) * J + r48 // H, 1.0, 0.0).astype(BF16)
    wl = mm(order, w_logit[...], 1, 0).astype(BF16)
    wl_t[...] = wl
    spread = head_spread()
    places = (
        ((m1, CELLS), (m2, PACK + CELLS)),
        ((m2, 2 * PACK + CELLS),),
        ((m2, 0),),
        ((m16, CELLS),),
        ((m16, CELLS + PACK),),
    )
    for message, start in ((m16, 0), (m2, PACK), (m1, 0)):
        message[pl.ds(start, CELLS), :] = cot[...]
    valid = [None]
    for k in range(K):
        valid.append((present[0, k] == 1) & (frame >= DISTANCES[k]))
    accum[pl.ds(0, COLS), :] = jnp.zeros((COLS, C), F32)
    accum[pl.ds(EXT - COLS, COLS), :] = jnp.zeros((COLS, C), F32)
    for r in range(ROWS):
        f = feats[rows_of(r), :]
        v = mm(f, w_value[...], 1, 0).astype(BF16)
        values[rows_of(r), :] = v
        logits = mm(wl, f, 1, 1)
        masked = [logits[0:H]]
        for k in range(K):
            part = logits[(k + 1) * H : (k + 2) * H]
            masked.append(jnp.where(valid[k + 1], part, -1e30))
        top = masked[0]
        for part in masked[1:]:
            top = jnp.maximum(top, part)
        expo = [jnp.exp(masked[0] - top)]
        for k in range(K):
            expo.append(jnp.where(valid[k + 1], jnp.exp(masked[k + 1] - top), 0.0))
        total = expo[0]
        for part in expo[1:]:
            total = total + part
        weights = [part / total for part in expo]
        attn[:, rows_of(r)] = jnp.concatenate(weights, axis=0)
        for k in range(K):
            head = jnp.concatenate(
                [
                    weights[k + 1],
                    col_off[k, r : r + 1, :].astype(F32),
                    row_off[k, r : r + 1, :].astype(F32),
                    fracs[0, k, r : r + 1, :].astype(F32),
                    fracs[1, k, r : r + 1, :].astype(F32),
                    jnp.zeros((4, COLS), F32),
                ],
                axis=0,
            )
            pack = head.astype(BF16)
            for message, start in places[k]:
                message[pl.ds(start + 16 * (r // 2), 16), pl.ds((r % 2) * COLS, COLS)] = pack
        wide = mm(weights[0].astype(BF16), spread, 0, 0)
        dm = mm(cot[rows_of(r), :], w_out[...], 1, 1).astype(BF16).astype(F32)
        vf = v.astype(F32)
        dattn[:, rows_of(r)] = head_sums(spread, dm * vf)
        accum[rows_of(r + 1), :] = (wide * dm).astype(BF16).astype(F32)
        mix[rows_of(r), :] = (wide * vf).astype(BF16)
    gwo[...] = mm(mix[...], cot[...], 0, 0)


def ext_body(values, low, high, w_value, ext):
    ext[pl.ds(0, COLS), :] = mm(low[...], w_value[...], 1, 0).astype(BF16)
    ext[pl.ds(COLS, CELLS), :] = values[...]
    ext[pl.ds(COLS + CELLS, COLS), :] = mm(high[...], w_value[...], 1, 0).astype(BF16)


def slot_body(
    cot_at, pack_at, message, ext, w_out, accum_in, gwo_in, dattn, accum, gwo, mix
):
    spread = head_spread()
    src = iota((COLS, COLS), 0).astype(F32)
    lane = iota((1, COLS), 1).astype(F32)
    accum[...] = accum_in[...]
    for r in range(ROWS):
        pack = message[pl.ds(pack_at + 16 * (r // 2), 16), pl.ds((r % 2) * COLS, COLS)]
        info = pack[8:16].astype(F32)
        c0 = lane + info[0:1]
        up = info[1:2] < -0.5
        a = info[2:3] * (1.0 / 64.0)
        b = info[3:4]
        near = 0.125 - a
        columns = jnp.where(src == c0, 8.0 - b, 0.0) + jnp.where(src == c0 + 1.0, b, 0.0)
        w0 = jnp.where(up, near, 0.0)
        w1 = jnp.where(up, a, near)
        w2 = jnp.where(up, 0.0, a)
        table = jnp.concatenate(
            [(columns * w0).astype(BF16), (columns * w1).astype(BF16), (columns * w2).astype(BF16)],
            axis=0,
        )
        window = pl.ds(r * COLS, 3 * COLS)
        taken = mm(table, ext[window, :], 0, 0).astype(BF16).astype(F32)
        wide = mm(pack[0:H], spread, 0, 0)
        cot = message[pl.ds(cot_at + r * COLS, COLS), :]
        dm = mm(cot, w_out[...], 1, 1).astype(BF16).astype(F32)
        dattn[:, rows_of(r)] = head_sums(spread, dm * taken)
        mix[rows_of(r), :] = (wide * taken).astype(BF16)
        accum[window, :] += mm(table, (wide * dm).astype(BF16), 1, 0)
    gwo[...] = gwo_in[...] + mm(mix[...], message[pl.ds(cot_at, CELLS), :], 0, 0)


def value_body(feats, low, high, accum, gwo, keep, send, rim_low, rim_high, dv):
    dv[...] = accum[...].astype(BF16)
    gwv = mm(feats[...], dv[pl.ds(COLS, CELLS), :], 0, 0)
    gwv = gwv + mm(low[...], dv[pl.ds(0, COLS), :], 0, 0)
    gwv = gwv + mm(high[...], dv[pl.ds(COLS + CELLS, COLS), :], 0, 0)
    rim_low[...] = dv[pl.ds(0, COLS), :]
    rim_high[...] = dv[pl.ds(COLS + CELLS, COLS), :]
    core = lax.axis_index("core")
    for mine in (0, 1):

        @pl.when(core == mine)
        def _():
            keep[...] = gwo[...] if mine == 0 else gwv
            send[...] = gwv if mine == 0 else gwo[...]


def logit_body(feats, attn, d0, d1, d2, d3, d4, d5, keep, came, dl_t, pay, dl):
    grads = (d0, d1, d2, d3, d4, d5)
    r48 = iota((H * J, COLS), 0)
    c48 = iota((H * J, COLS), 1)
    order = jnp.where(c48 == (r48 % H) * J + r48 // H, 1.0, 0.0).astype(BF16)
    weights = [attn[pl.ds(j * H, H), :] for j in range(J)]
    terms = [grads[j][...] for j in range(J)]
    mean = weights[0] * terms[0]
    for j in range(1, J):
        mean = mean + weights[j] * terms[j]
    low = jnp.concatenate(
        [weights[j] * (terms[j] - mean) for j in range(J)], axis=0
    ).astype(BF16)
    dl_t[...] = low
    for r in range(ROWS):
        dl[rows_of(r), :] = mm(low[:, r * COLS : (r + 1) * COLS], order, 0, 0).astype(BF16)
    pay[:, pl.ds(0, C)] = keep[...] + came[...]
    pay[:, pl.ds(C, COLS)] = mm(feats[...], dl[...], 0, 0)


def feats_body(cot, w_value, wl_t, dl_t, accum, from_prev, from_next, grad_feats):
    for r in range(ROWS):
        center = accum[rows_of(r + 1), :]
        if r == 0:
            center = center + from_prev[...].astype(F32)
        if r == ROWS - 1:
            center = center + from_next[...].astype(F32)
        out = cot[rows_of(r), :].astype(F32) + mm(center.astype(BF16), w_value[...], 1, 1)
        out = out + mm(dl_t[:, rows_of(r)], wl_t[...], 0, 0)
        grad_feats[rows_of(r), :] = out.astype(BF16)


VM = pl.BlockSpec(memory_space=pltpu.VMEM)
SM = pl.BlockSpec(memory_space=pltpu.SMEM)
HB = pl.BlockSpec(memory_space=pltpu.HBM)


def sds(shape, dtype):
    return jax.ShapeDtypeStruct(shape, dtype)


def cost(flops, nbytes):
    return pl.CostEstimate(flops=flops, bytes_accessed=nbytes, transcendentals=0)


PARAMS = pltpu.CompilerParams(vmem_limit_bytes=24 * 1024 * 1024)


def prep(present, feats, cot, w_value, w_logit, w_out, row_off, col_off, fracs):
    return pl.pallas_call(
        prep_body,
        name="prep",
        out_shape=(
            sds((CELLS, C), BF16),
            sds((H * J, CELLS), F32),
            sds((CELLS + 2 * PACK, C), BF16),
            sds((CELLS + 3 * PACK, C), BF16),
            sds((CELLS + PACK, C), BF16),
            sds((H, CELLS), F32),
            sds((EXT, C), F32),
            sds((C, C), F32),
            sds((H * J, C), BF16),
        ),
        in_specs=[SM] + [HB] * 8,
        out_specs=(VM,) * 9,
        scratch_shapes=[
            pltpu.VMEM((CELLS, C), BF16),
            pltpu.VMEM((CELLS, C), BF16),
            pltpu.VMEM((CELLS, C), BF16),
            pltpu.VMEM((C, C), BF16),
            pltpu.VMEM((H * J, C), BF16),
            pltpu.VMEM((C, C), BF16),
            pltpu.VMEM((K, ROWS, COLS), jnp.int32),
            pltpu.VMEM((K, ROWS, COLS), jnp.int32),
            pltpu.VMEM((2, K, ROWS, COLS), jnp.int32),
            pltpu.SemaphoreType.DMA((8,)),
        ],
        compiler_params=PARAMS,
        cost_estimate=cost(10**9, 4 * 10**6),
    )(
        present,
        *(
            pltpu.with_memory_space_constraint(x, pltpu.HBM)
            for x in (feats, cot, w_value, w_logit, w_out, row_off, col_off, fracs)
        ),
    )


def slot_call(cot_at, pack_at, message, ext, w_out, accum, gwo):
    return pl.pallas_call(
        functools.partial(slot_body, cot_at, pack_at),
        name="slot",
        out_shape=(sds((H, CELLS), F32), sds((EXT, C), F32), sds((C, C), F32)),
        in_specs=[VM] * 5,
        out_specs=(VM,) * 3,
        scratch_shapes=[pltpu.VMEM((CELLS, C), BF16)],
        input_output_aliases={3: 1, 4: 2},
        compiler_params=PARAMS,
        cost_estimate=cost(10**9, 4 * 10**6),
    )(message, ext, w_out, accum, gwo)


def plain(body, outs, scratch, *args):
    return pl.pallas_call(
        body,
        out_shape=outs,
        in_specs=[VM] * len(args),
        out_specs=(VM,) * len(outs),
        scratch_shapes=scratch,
        compiler_params=PARAMS,
        cost_estimate=cost(2 * 10**8, 2 * 10**6),
    )(*args)


def size(axis):
    return math.prod(lax.axis_size(a) for a in axis) if isinstance(axis, tuple) else lax.axis_size(axis)


def shifted(value, axis, steps):
    count = size(axis)
    initial, last = (max(0, -steps), min(count, count - steps))
    return lax.ppermute(value, axis, [(source, source + steps) for source in range(initial, last)])


def layer(feats, cotangent, w_value, w_logit, w_out, row_offsets, col_offsets, fractions, present):
    inputs = feats.reshape(CELLS, C)
    grad_out = cotangent.reshape(CELLS, C)
    count = size(TM)
    low = shifted(inputs[CELLS - COLS :], "band", 1)
    high = shifted(inputs[:COLS], "band", -1)
    values, attn, m16, m2, m1, d0, accum, gwo, wl_t = prep(
        present, inputs, grad_out, w_value, w_logit.T, w_out, row_offsets[0], col_offsets[0], fractions[0]
    )
    messages = [None] * K
    messages[1] = shifted(m2, TM, -2)
    messages[4] = shifted(m16, TM, -16)
    near = lax.ppermute(m1, TM, [(i, i - 1) for i in range(1, count, 2)])
    (ext,) = plain(ext_body, (sds((EXT, C), BF16),), [], values, low, high, w_value)
    messages[2] = shifted(messages[1][: CELLS + PACK], TM, -2)
    far = lax.ppermute(
        messages[1][PACK : CELLS + 2 * PACK], TM, [(i, i + 1) for i in range(0, count, 2)]
    )
    messages[0] = near + far
    messages[3] = shifted(m16[: CELLS + PACK], TM, -8)
    places = ((0, CELLS), (PACK, CELLS + 2 * PACK), (PACK, 0), (0, CELLS), (0, CELLS + PACK))
    grads = [None] * K
    back = [None] * K
    for k in SLOTS:
        grads[k], accum, gwo = slot_call(*places[k], messages[k], ext, w_out, accum, gwo)
        back[k] = shifted(grads[k], TM, DISTANCES[k])
    swap = [(0, 1), (1, 0)]
    square = sds((C, C), F32)
    rim = sds((COLS, C), BF16)
    keep, send, rim_low, rim_high = plain(
        value_body, (square, square, rim, rim), [pltpu.VMEM((EXT, C), BF16)],
        inputs, low, high, accum, gwo,
    )
    came = lax.ppermute(send, "core", swap)
    dl_t, pay = plain(
        logit_body, (sds((H * J, CELLS), BF16), sds((C, PAY), F32)),
        [pltpu.VMEM((CELLS, COLS), BF16)],
        inputs, attn, d0, *back, keep, came,
    )
    both = ("pair", "band")
    count = size(both)
    share = C // count
    pieces = lax.all_to_all(pay, both, 0, 0, tiled=True)
    from_next = shifted(rim_low, "band", -1)
    from_prev = shifted(rim_high, "band", 1)
    mine = jnp.sum(pieces.reshape(count, share, PAY), axis=0)
    spread = jnp.broadcast_to(mine[None], (count, share, PAY)).reshape(C, PAY)
    own = lax.all_to_all(spread, both, 0, 0, tiled=True)
    (grad_feats,) = plain(
        feats_body, (sds((CELLS, C), BF16),), [],
        grad_out, w_value, wl_t, dl_t, accum, from_prev, from_next,
    )
    other = lax.ppermute(own, "core", swap)
    first = lax.axis_index("core") == 0
    own_square, other_square = own[:, :C], other[:, :C]
    gwl = (own[:, C:] + other[:, C:])[:, : H * J]
    return (
        grad_feats.reshape(feats.shape),
        jnp.where(first, other_square, own_square),
        gwl,
        jnp.where(first, own_square, other_square),
    )


def solution(mesh):
    frames, bands = mesh.shape["tm"], mesh.shape["band"]
    inner = jax.sharding.Mesh(
        np.asarray(mesh.devices).reshape(frames // 2, 2, bands), ("pair", "core", "band")
    )
    placed = (
        P(TM, "band", None, None),
        P(TM, "band", None, None),
        P(),
        P(),
        P(),
        P(TM, None, "band", None),
        P(TM, None, "band", None),
        P(TM, None, None, "band", None),
        P(TM, None),
    )
    return jax.shard_map(
        layer,
        mesh=inner,
        in_specs=placed,
        out_specs=(P(TM, "band", None, None), P(), P(), P()),
        check_vma=False,
    )
```
